32 devices in a mesh: groups: 2 (over y), seq: 4 (over z), head: 2 (over x), rep: 2 (over core).
Axes of the slice: x: 2, y: 2, z: 4, core: 2. Of those that a mesh axis runs over, the one named last changes fastest.
Arguments:
- queries: bfloat16 [32768, 16, 128], P(('groups', 'seq'), ('head', 'rep')), parts along dimension 0, may hold values from -8 to 8
- keys: bfloat16 [32768, 128], P(('groups', 'seq')), parts along dimension 0, may hold values from -6 to 6
- values: bfloat16 [32768, 128], P(('groups', 'seq')), parts along dimension 0, may hold values from -6 to 6
- query_maps: bfloat16 [32, 128, 128], P(('groups', 'head', 'rep')), parts along dimension 0, may hold values from -0.5 to 0.5
- key_map: bfloat16 [256, 128], P('groups'), parts along dimension 0, may hold values from -0.046875 to 0.046875
- linear_cotangent: bfloat16 [32768, 16, 128], P(('groups', 'seq'), ('head', 'rep')), parts along dimension 0, may hold values from -0.046875 to 0.046875
Outputs:
- softmax_out: bfloat16 [32768, 16, 128], P(('groups', 'seq'), ('head', 'rep')), parts along dimension 0
- linear_out: bfloat16 [32768, 16, 128], P(('groups', 'seq'), ('head', 'rep')), parts along dimension 0
- map_gradient: float32 [256, 16, 128], P(('groups', 'seq'), ('head', 'rep')), parts along dimension 0
The draws below stay inside these ranges and needn't reach their ends.
There are 2 independent parts, one for each index of `groups`. The reference program is written for one: setup_inputs(seed, part) draws one part's arguments, and reference() takes and returns one part's arrays. A program takes and returns all parts, laid end to end along the dimension named above; each array names one. Nothing has to cross between parts.
All inputs are finite; a program needn't handle non-finite values.
Results may differ from the reference program's by a relative error of at most 0.0058.
Values may be sent and summed in bfloat16 or wider, within the bound.
A program may use at most 128 MiB of HBM per device.

```python
import jax
import jax.numpy as jnp
from jax import lax

H = 16
HD = 128
W = 512
TOKENS = 16384


def draw_keys(key, part):
    drawn = jnp.clip(jax.random.normal(jax.random.fold_in(key, 11), (TOKENS, HD), jnp.float32), -6.0, 6.0)
    return drawn.astype(jnp.bfloat16)


def draw_queries(key, part):
    drawn = jnp.clip(jax.random.normal(jax.random.fold_in(key, 21), (TOKENS, H, HD), jnp.float32), -6.0, 6.0)
    return drawn.astype(jnp.bfloat16)


def block_scale(own_key, extent, cuts, least, largest):
    gain, own = 1.0, jax.random.fold_in(own_key, 6)
    for position, blocks in cuts:
        draws = jnp.exp(jax.random.uniform(jax.random.fold_in(own, position), (blocks,), jnp.float32, least / len(cuts), largest / len(cuts)))
        gain = gain * jnp.repeat(draws, extent[position] // blocks).reshape([-1 if axis == position else 1 for axis in range(len(extent))])
    return gain


def normal_values(own_key, shape, scale, most, cuts=(), kind=jnp.bfloat16):
    values = scale * jax.random.normal(own_key, shape, jnp.float32)
    if cuts:
        values = values * block_scale(own_key, shape, cuts, -0.22, 0.18)
    return jnp.clip(values, -most, most).astype(kind)


def setup_inputs(seed: int = 0, part: int = 0) -> dict:
    arg_keys = jax.random.split(jax.random.key(seed), 7)
    part_splits = jax.random.split(jax.random.fold_in(arg_keys[6], part), 7)
    queries = draw_queries(jax.random.fold_in(jax.random.fold_in(arg_keys[6], part), 71), part)
    keys = draw_keys(jax.random.fold_in(jax.random.fold_in(arg_keys[6], part), 71), part)
    values = normal_values(part_splits[2], (TOKENS, HD), 1.0, 6.0, ((0, 4),))
    query_maps = normal_values(part_splits[3], (H, HD, HD), HD ** -0.5, 0.5, ((0, 4),))
    key_map = normal_values(part_splits[4], (HD, HD), (HD * HD) ** -0.5, 0.046875)
    linear_cotangent = normal_values(part_splits[5], (TOKENS, H, HD), (1.0 / TOKENS ** 0.5), 0.046875, ((0, 4), (1, 4)))
    return {"queries": queries, "keys": keys, "values": values, "query_maps": query_maps, "key_map": key_map, "linear_cotangent": linear_cotangent}


def window_block(block_index, start_state, tensors):
    queries, keys_ext, values_ext, query_features, key_features, values, cotangent = tensors
    highest_precision = lax.Precision.HIGHEST
    first_row = block_index * W
    head_dim = keys_ext.shape[1]
    query_block = lax.dynamic_slice_in_dim(queries, first_row, W, 0).astype(jnp.float32)
    key_window = lax.dynamic_slice_in_dim(keys_ext, first_row, 2 * W, 0).astype(jnp.float32)
    value_window = lax.dynamic_slice_in_dim(values_ext, first_row, 2 * W, 0).astype(jnp.float32)
    query_pos = first_row + jnp.arange(W, dtype=jnp.int32)
    key_pos = first_row - W + jnp.arange(2 * W, dtype=jnp.int32)
    spacing = query_pos[:, None] - key_pos[None, :]
    allowed = (spacing >= 0) & (spacing < W) & (key_pos[None, :] >= 0)
    scores = jnp.einsum('whd,kd->hwk', query_block, key_window, precision=highest_precision) * head_dim ** (-0.5)
    scores = jnp.where(allowed[None], scores, -1e+30)
    highest = lax.optimization_barrier(jnp.max(scores, axis=2, keepdims=True))
    shifted_exp = jnp.exp(scores - highest)
    weights = (shifted_exp / lax.optimization_barrier(jnp.sum(shifted_exp, axis=2, keepdims=True))).astype(jnp.bfloat16)
    soft_block = jnp.einsum('hwk,kd->whd', weights.astype(jnp.float32), value_window, precision=highest_precision).astype(jnp.bfloat16)
    feature_block = lax.dynamic_slice_in_dim(query_features, first_row, W, 0).astype(jnp.float32)
    key_block = lax.dynamic_slice_in_dim(key_features, first_row, W, 0).astype(jnp.float32)
    value_block = lax.dynamic_slice_in_dim(values, first_row, W, 0).astype(jnp.float32)
    cotangent_block = lax.dynamic_slice_in_dim(cotangent, first_row, W, 0).astype(jnp.float32)
    causal = jnp.arange(W)[:, None] >= jnp.arange(W)[None, :]
    factor = lax.rsqrt((query_pos + 1).astype(jnp.float32))[:, None, None]
    linear_scores = jnp.where(causal[None], jnp.einsum('whf,sf->hws', feature_block, key_block, precision=highest_precision), 0.0).astype(jnp.bfloat16)
    inside = jnp.einsum('hws,sd->whd', linear_scores.astype(jnp.float32), value_block, precision=highest_precision)
    carried = jnp.einsum('whf,fd->whd', feature_block, start_state, precision=highest_precision)
    linear_block = (factor * (inside + carried)).astype(jnp.bfloat16)
    back_scores = jnp.where(causal[None], jnp.einsum('whd,sd->hws', cotangent_block, value_block, precision=highest_precision), 0.0).astype(jnp.bfloat16)
    back_inside = jnp.einsum('hws,sf->whf', back_scores.astype(jnp.float32), key_block, precision=highest_precision)
    back_carried = jnp.einsum('whd,fd->whf', cotangent_block, start_state, precision=highest_precision)
    feature_gradient = (factor * (back_inside + back_carried)).astype(jnp.bfloat16)
    return (soft_block, linear_block, feature_gradient)

def reference(queries, keys, values, query_maps, key_map, linear_cotangent):
    token_count = keys.shape[0]
    head_dim = keys.shape[1]
    head_count = queries.shape[1]
    block_count = token_count // W
    key_features = jnp.dot(keys, key_map, preferred_element_type=jnp.float32).astype(jnp.bfloat16)
    query_features = jnp.einsum('thd,hdf->thf', queries.astype(jnp.float32), query_maps.astype(jnp.float32), precision=lax.Precision.HIGHEST).astype(jnp.bfloat16)
    block_states = jnp.einsum('bwf,bwd->bfd', key_features.reshape(block_count, W, head_dim).astype(jnp.float32), values.reshape(block_count, W, head_dim).astype(jnp.float32), precision=lax.Precision.HIGHEST)
    running = jnp.cumsum(block_states, axis=0)
    starts = jnp.concatenate([jnp.zeros_like(block_states[:1]), running[:-1]], axis=0)
    padding = jnp.zeros((W, head_dim), keys.dtype)
    keys_ext = jnp.concatenate([padding, keys], axis=0)
    values_ext = jnp.concatenate([padding, values], axis=0)
    tensors = (queries, keys_ext, values_ext, query_features, key_features, values, linear_cotangent)

    def one_block(block_item):
        return window_block(block_item[0], block_item[1], tensors)
    soft_parts, linear_parts, gradient_parts = lax.map(one_block, (jnp.arange(block_count, dtype=jnp.int32), starts))
    softmax_out = soft_parts.reshape(token_count, head_count, head_dim)
    linear_out = linear_parts.reshape(token_count, head_count, head_dim)
    feature_gradient = gradient_parts.reshape(token_count, head_count, head_dim)
    map_gradient = jnp.einsum('the,thf->ehf', queries.astype(jnp.float32), feature_gradient.astype(jnp.float32), precision=lax.Precision.HIGHEST)
    return (softmax_out, linear_out, map_gradient)
```

```python
import functools

import jax
import jax.numpy as jnp
from jax import lax
from jax.experimental import pallas as pl
from jax.experimental.pallas import tpu as pltpu
from jax.sharding import PartitionSpec as P

W = 512
TILE = 128
MIDS = W // TILE
ONES = 16
MESH = pl.DeviceIdType.MESH
F32 = jnp.float32
BF16 = jnp.bfloat16


def nt(a, b):
    return lax.dot_general(a, b, (((1,), (1,)), ((), ())), preferred_element_type=F32)


def nn(a, b):
    return jnp.dot(a, b, preferred_element_type=F32)


def beside(parts):
    return parts[0] if len(parts) == 1 else jnp.concatenate(parts, 1)


def below(parts):
    return parts[0] if len(parts) == 1 else jnp.concatenate(parts, 0)


def later_key(heads):
    shape = (TILE, heads * TILE)
    return lax.broadcasted_iota(jnp.int32, shape, 0) > lax.broadcasted_iota(jnp.int32, shape, 1) % TILE


def heads_apart(ref):
    return pltpu.einshape("tha->hta", ref[...])


def tile_of(x, tile):
    rows = slice(tile * TILE, (tile + 1) * TILE)
    return below([x[h, rows] for h in range(x.shape[0])])


def head_cols(x):
    return [x[:, h : h + TILE] for h in range(0, x.shape[1], TILE)]


def heads_together(tiles):
    heads = tiles[0].shape[1] // TILE
    rows = [below([head_cols(t)[h].T for t in tiles])[None] for h in range(heads)]
    return pltpu.einshape("hta->tha", below(rows))


def scale_of(rank, tokens_here, first, heads):
    token = lax.broadcasted_iota(jnp.int32, (1, TILE), 1) + (rank * tokens_here + first + 1)
    return beside([lax.rsqrt(token.astype(F32))] * heads)


def softmax_weights(scores, ahead, hd):
    scale = hd ** (-0.5) * 1.4426950408889634
    parts = [scores[j * TILE : (j + 1) * TILE] for j in range(MIDS + 1)]
    kept = [jnp.where(ahead, parts[0], parts[MIDS])] + parts[1:MIDS]
    highest = jnp.max(functools.reduce(jnp.maximum, kept), axis=0, keepdims=True)
    kept = [jnp.exp2((p - highest) * scale) for p in kept]
    return below(
        [jnp.where(ahead, kept[0], 0.0).astype(BF16)]
        + [p.astype(BF16) for p in kept[1:]]
        + [jnp.where(ahead, 0.0, kept[0]).astype(BF16)]
    )


def softmax_tiles(q_ref, k_ext, v_ext, out_ref, first_tile, tiles, ahead):
    hd = q_ref.shape[2]
    q = heads_apart(q_ref)

    def scores(t):
        first = pl.multiple_of((first_tile + t) * TILE, TILE)
        return nt(k_ext[pl.ds(first, W + TILE), :], tile_of(q, t))

    def output(t, weights):
        values = beside([v_ext[first_tile + t + j] for j in range(MIDS + 1)])
        out = nn(values, weights)
        return (out[:hd] * (1.0 / out[hd : hd + 1])).astype(BF16)

    done, weights = [], None
    now = scores(0)
    for t in range(tiles):
        after = scores(t + 1) if t + 1 < tiles else None
        fresh = softmax_weights(now, ahead, hd)
        if weights is not None:
            done.append(output(t - 1, weights))
        now, weights = after, fresh
    done.append(output(tiles - 1, weights))
    out_ref[...] = heads_together(done)


def first_kernel(
    count, tokens_here, tiles, before, middle, steps,
    q_ref, c_ref, k_ref, v_ref, key_map_ref,
    soft_ref, kf_ref, vt_ref, prefix_ref, mine_ref,
    k_ext, v_ext, kft, local_sum, sums, halo, state, grad, pieces, pieces16, slots,
    sum_send, sum_recv, halo_send, halo_recv, piece_send, piece_recv,
):
    step = pl.program_id(0)
    rank = lax.axis_index("seq")
    heads, hd = q_ref.shape[1:]
    blocks = tokens_here // TILE
    share = hd // count
    barrier = pltpu.get_barrier_semaphore()

    def halo_copy(i):
        return pltpu.make_async_remote_copy(
            src_ref=(k_ref, v_ref)[i].at[pl.ds(tokens_here - W, W)],
            dst_ref=halo.at[i],
            send_sem=halo_send.at[i],
            recv_sem=halo_recv.at[i],
            device_id={"seq": rank + 1},
            device_id_type=MESH,
        )

    def sum_copy(k):
        return pltpu.make_async_remote_copy(
            src_ref=local_sum,
            dst_ref=sums.at[k - 1],
            send_sem=sum_send.at[k - 1],
            recv_sem=sum_recv.at[k - 1],
            device_id={"seq": rank + k},
            device_id_type=MESH,
        )

    def piece_copy(k):
        target = lax.rem(rank + k, count)
        return pltpu.make_async_remote_copy(
            src_ref=pieces16.at[target],
            dst_ref=slots.at[k - 1],
            send_sem=piece_send.at[k - 1],
            recv_sem=piece_recv.at[k - 1],
            device_id={"seq": target},
            device_id_type=MESH,
        )

    @pl.when(step == 0)
    def _():
        for k in range(1, count):
            pl.semaphore_signal(
                barrier, inc=1, device_id={"seq": lax.rem(rank + k, count)}, device_id_type=MESH
            )
        key_map_t = key_map_ref[...].astype(F32).T.astype(BF16)
        kft[...] = nt(key_map_t, k_ref[...]).astype(BF16)
        local_sum[...] = nn(kft[...], v_ref[...]).astype(BF16)
        kf_ref[...] = nn(k_ref[...], key_map_ref[...]).astype(BF16)
        k_ext[W:] = k_ref[...]
        for b in range(blocks):
            turned = v_ref[b * TILE : (b + 1) * TILE, :].T
            vt_ref[b] = turned
            v_ext[MIDS + b, :hd] = turned
        v_ext[MIDS:, hd:] = jnp.ones((blocks, ONES, TILE), BF16)
        grad[...] = jnp.zeros_like(grad)

    @pl.when(step == 1)
    def _():
        pl.semaphore_wait(barrier, count - 1)
        for k in range(1, count):
            @pl.when(rank + k < count)
            def _():
                sum_copy(k).start()
        @pl.when(rank + 1 < count)
        def _():
            halo_copy(0).start()
            halo_copy(1).start()

    @pl.when(step == before)
    def _():
        state[...] = jnp.zeros_like(state)
        for k in range(1, count):
            @pl.when(rank + k < count)
            def _():
                sum_copy(k).wait_send()
            @pl.when(rank >= k)
            def _():
                sum_copy(k).wait_recv()
                state[...] += sums[k - 1].astype(F32)
        prefix_ref[...] = state[...].T

    @pl.when(step == before + middle)
    def _():
        for h in range(heads):
            turned = grad[h].T
            for p in range(count):
                piece = turned[p * share : (p + 1) * share]
                pieces[p, :, h * hd : (h + 1) * hd] = piece
                pieces16[p, :, h * hd : (h + 1) * hd] = piece.astype(BF16)
        for k in range(1, count):
            piece_copy(k).start()

    @pl.when(step == steps - 1)
    def _():
        @pl.when(rank + 1 < count)
        def _():
            halo_copy(0).wait_send()
            halo_copy(1).wait_send()
        @pl.when(rank >= 1)
        def _():
            halo_copy(0).wait_recv()
            halo_copy(1).wait_recv()
            k_ext[:W] = halo[0]
            for b in range(MIDS):
                v_ext[b, :hd] = halo[1, b * TILE : (b + 1) * TILE, :].T
                v_ext[b, hd:] = jnp.ones((ONES, TILE), BF16)
        @pl.when(rank == 0)
        def _():
            k_ext[:W] = jnp.broadcast_to(k_ref[0:1, :], (W, hd))
            v_ext[:MIDS] = jnp.zeros((MIDS,) + v_ext.shape[1:], BF16)

    ahead = later_key(heads)

    @pl.when((step < before) | (step >= before + middle))
    def _():
        place = jnp.where(step < before, steps - middle - 1 - step, steps - 1 - step)
        softmax_tiles(q_ref, k_ext, v_ext, soft_ref, place * tiles, tiles, ahead)

    @pl.when((step >= before) & (step < before + middle))
    def _():
        base = (step - before) * tiles
        q = heads_apart(q_ref)
        c = heads_apart(c_ref)
        starts = []
        now = state[...]
        for t in range(tiles):
            starts.append(now.astype(BF16))
            first = pl.multiple_of((base + t) * TILE, TILE)
            now = now + nn(kft[:, pl.ds(first, TILE)], v_ref[pl.ds(first, TILE), :])
        state[...] = now

        turned = [tile_of(c, t).T for t in range(tiles)]

        def scores(t):
            first = pl.multiple_of((base + t) * TILE, TILE)
            back = nn(v_ref[pl.ds(first, TILE), :], turned[t])
            return jnp.where(ahead, 0.0, back).astype(BF16)

        def gradient(t, back):
            first = pl.multiple_of((base + t) * TILE, TILE)
            out = nn(beside([kft[:, pl.ds(first, TILE)], starts[t]]), below([back, turned[t]]))
            return (out * scale_of(rank, tokens_here, first, heads)).astype(BF16)

        backs = [scores(t) for t in range(tiles)]
        found = [head_cols(gradient(t, backs[t])) for t in range(tiles)]
        for h in range(heads):
            grad[h] += nn(beside([found[t][h] for t in range(tiles)]), q[h])

    @pl.when(step == steps - 1)
    def _():
        total = pieces[rank]
        for k in range(1, count):
            piece_copy(k).wait()
            total = total + slots[k - 1].astype(F32)
        mine_ref[...] = total


def last_kernel(
    tokens_here, tiles, steps,
    q_ref, soft_in_ref, maps_ref, kf_ref, vt_ref, prefix_ref, mine_in_ref,
    soft_ref, linear_ref, mine_ref,
    maps_t, state,
):
    step = pl.program_id(0)
    rank = lax.axis_index("seq")
    heads, hd = q_ref.shape[1:]

    @pl.when(step == 0)
    def _():
        for h in range(heads):
            maps_t[h] = maps_ref[h].T
            mine_ref[:, h, :] = mine_in_ref[:, h * hd : (h + 1) * hd]
        state[...] = prefix_ref[...]

    soft_ref[...] = soft_in_ref[...]
    ahead = later_key(heads)
    q = heads_apart(q_ref)
    base = step * tiles
    starts = []
    now = state[...]
    for t in range(tiles):
        starts.append(now.astype(BF16))
        first = pl.multiple_of((base + t) * TILE, TILE)
        now = now + nn(vt_ref[base + t], kf_ref[pl.ds(first, TILE), :])
    state[...] = now

    features = [nt(maps_t[h], q[h]).astype(BF16) for h in range(heads)]
    turned = [beside([head_cols(f)[t] for f in features]) for t in range(tiles)]

    def scores(t):
        first = pl.multiple_of((base + t) * TILE, TILE)
        return jnp.where(ahead, 0.0, nn(kf_ref[pl.ds(first, TILE), :], turned[t])).astype(BF16)

    def output(t, inside):
        first = (base + t) * TILE
        out = nn(beside([vt_ref[base + t], starts[t]]), below([inside, turned[t]]))
        return (out * scale_of(rank, tokens_here, first, heads)).astype(BF16)

    insides = [scores(t) for t in range(tiles)]
    linear_ref[...] = heads_together([output(t, insides[t]) for t in range(tiles)])


def per_device(queries, keys, values, query_maps, key_map, linear_cotangent):
    tokens_here, hd = keys.shape
    heads = queries.shape[1]
    count = lax.axis_size("seq")
    share = hd // count
    tiles = 4
    step_tokens = TILE * tiles
    middle = tokens_here // step_tokens
    before = middle // 2
    steps = 2 * middle
    blocks = tokens_here // TILE
    once = lambda a: pl.BlockSpec(a.shape, lambda i: (0,) * len(a.shape), pipeline_mode=pl.Buffered(1))
    block = lambda index: pl.BlockSpec((step_tokens, heads, hd), lambda i: (index(i), 0, 0))
    dma = pltpu.SemaphoreType.DMA

    def soft_place(i):
        held = jnp.where(i < before + middle, middle - before, steps - 1 - i)
        return jnp.where(i < before, middle - 1 - i, held)

    def middle_place(i):
        return jnp.clip(i - before, 0, middle - 1)

    def query_place(i):
        return jnp.where((i >= before) & (i < before + middle), i - before, soft_place(i))

    rows16 = jax.ShapeDtypeStruct((tokens_here, heads, hd), BF16)
    kf16 = jax.ShapeDtypeStruct((tokens_here, hd), BF16)
    vt16 = jax.ShapeDtypeStruct((blocks, hd, TILE), BF16)
    square = jax.ShapeDtypeStruct((hd, hd), F32)
    piece = jax.ShapeDtypeStruct((share, heads * hd), F32)
    soft, key_features, values_t, prefix, mine = pl.pallas_call(
        functools.partial(first_kernel, count, tokens_here, tiles, before, middle, steps),
        grid=(steps,),
        in_specs=[block(query_place), block(middle_place)] + [once(a) for a in (keys, values, key_map)],
        out_specs=[block(soft_place)] + [once(a) for a in (kf16, vt16, square, piece)],
        out_shape=[rows16, kf16, vt16, square, piece],
        scratch_shapes=[
            pltpu.VMEM((tokens_here + W, hd), BF16),
            pltpu.VMEM((blocks + MIDS, hd + ONES, TILE), BF16),
            pltpu.VMEM((hd, tokens_here), BF16),
            pltpu.VMEM((hd, hd), BF16),
            pltpu.VMEM((count - 1, hd, hd), BF16),
            pltpu.VMEM((2, W, hd), BF16),
            pltpu.VMEM((hd, hd), F32),
            pltpu.VMEM((heads, hd, hd), F32),
            pltpu.VMEM((count, share, heads * hd), F32),
            pltpu.VMEM((count, share, heads * hd), BF16),
            pltpu.VMEM((count - 1, share, heads * hd), BF16),
            dma((count - 1,)), dma((count - 1,)), dma((2,)), dma((2,)), dma((count - 1,)), dma((count - 1,)),
        ],
        compiler_params=pltpu.CompilerParams(
            dimension_semantics=("arbitrary",), collective_id=0, has_side_effects=True
        ),
        name="softmax_and_gradient",
    )(queries, linear_cotangent, keys, values, key_map)

    along = block(lambda i: i)
    small = (query_maps, key_features, values_t, prefix, mine)
    final = jax.ShapeDtypeStruct((share, heads, hd), F32)
    return pl.pallas_call(
        functools.partial(last_kernel, tokens_here, tiles, middle),
        grid=(middle,),
        in_specs=[along, along] + [once(a) for a in small],
        out_specs=[along, along, once(final)],
        out_shape=[rows16, rows16, final],
        scratch_shapes=[pltpu.VMEM((heads, hd, hd), BF16), pltpu.VMEM((hd, hd), F32)],
        compiler_params=pltpu.CompilerParams(dimension_semantics=("arbitrary",)),
        name="linear",
    )(queries, soft, *small)


def solution(mesh):
    rows = P(("groups", "seq"), ("head", "rep"), None)
    return jax.shard_map(
        per_device,
        mesh=mesh,
        in_specs=(
            rows,
            P(("groups", "seq"), None),
            P(("groups", "seq"), None),
            P(("groups", "head", "rep"), None, None),
            P("groups", None),
            rows,
        ),
        out_specs=(rows, rows, rows),
        check_vma=False,
    )
```

```python
import functools

import jax
import jax.numpy as jnp
from jax import lax
from jax.experimental import pallas as pl
from jax.experimental.pallas import tpu as pltpu
from jax.sharding import PartitionSpec as P

W = 512
TILE = 128
MIDS = W // TILE
ONES = 16
MESH = pl.DeviceIdType.MESH
F32 = jnp.float32
BF16 = jnp.bfloat16


def nt(a, b):
    return lax.dot_general(a, b, (((1,), (1,)), ((), ())), preferred_element_type=F32)


def nn(a, b):
    return jnp.dot(a, b, preferred_element_type=F32)


def beside(parts):
    return parts[0] if len(parts) == 1 else jnp.concatenate(parts, 1)


def below(parts):
    return parts[0] if len(parts) == 1 else jnp.concatenate(parts, 0)


def later_key(heads):
    shape = (TILE, TILE)
    one = lax.broadcasted_iota(jnp.int32, shape, 0) > lax.broadcasted_iota(jnp.int32, shape, 1)
    return beside([one] * heads)


def later_key_in_band(heads):
    shape = (TILE // heads, TILE)
    return lax.broadcasted_iota(jnp.int32, shape, 0) > lax.broadcasted_iota(jnp.int32, shape, 1) // heads


def columns(x):
    return [x[:, h : h + TILE] for h in range(0, x.shape[1], TILE)]


def at_tile(tile, rows=TILE):
    return pl.ds(pl.multiple_of(tile * rows, rows), rows)


def head_rows(ref, tile, heads):
    if heads == 1:
        return [ref[at_tile(tile), :]]
    own = ref.at[at_tile(tile, TILE * heads), :]
    return [own[pl.ds(h, TILE, stride=heads), :] for h in range(heads)]


def scale_of(before, tile, heads):
    token = lax.broadcasted_iota(jnp.int32, (1, TILE), 1) + (before + tile * TILE + 1)
    return beside([lax.rsqrt(token.astype(F32))] * heads)


def softmax_weights(scores, heads, hd):
    scale = hd ** (-0.5) * 1.4426950408889634
    ahead = later_key_in_band(heads)
    span = TILE // heads
    found = []
    for g, own in enumerate(columns(scores)):
        parts = [own[j * TILE : (j + 1) * TILE] for j in range(MIDS + 1)]
        a, b = g * span, (g + 1) * span
        edge = [parts[MIDS][:a]] * (a > 0) + [jnp.where(ahead, parts[0][a:b], parts[MIDS][a:b])]
        kept = [below(edge + [parts[0][b:]] * (b < TILE))] + parts[1:MIDS]
        highest = jnp.max(functools.reduce(jnp.maximum, kept), axis=0, keepdims=True)
        kept = [jnp.exp2((p - highest) * scale) for p in kept]
        edge = kept[0]
        old = [jnp.zeros((a, TILE), BF16)] * (a > 0) + [jnp.where(ahead, edge[a:b], 0.0).astype(BF16)]
        new = [jnp.where(ahead, 0.0, edge[a:b]).astype(BF16)]
        if a > 0:
            new = [edge[:a].astype(BF16)] + new
        if b < TILE:
            old = old + [edge[b:].astype(BF16)]
            new = new + [jnp.zeros((TILE - b, TILE), BF16)]
        found.append(below(old + [p.astype(BF16) for p in kept[1:]] + new))
    return beside(found)


def softmax_tiles(q_ref, k_ext, v_ext, out_ref, first_tile, tiles, heads):
    hd = q_ref.shape[1]
    rows = TILE * heads

    def scores(t):
        keys = k_ext[pl.ds(pl.multiple_of((first_tile + t) * TILE, TILE), W + TILE), :]
        return nt(keys, q_ref[at_tile(first_tile + t, rows), :])

    def output(t, weights):
        values = beside([v_ext[first_tile + t + j] for j in range(MIDS + 1)])
        out = nn(values, weights)
        out_ref[at_tile(first_tile + t, rows), :] = (out[:hd] * (1.0 / out[hd : hd + 1])).astype(BF16).T

    weights, now = None, scores(0)
    for t in range(tiles):
        after = scores(t + 1) if t + 1 < tiles else None
        fresh = softmax_weights(now, heads, hd)
        if weights is not None:
            output(t - 1, weights)
        now, weights = after, fresh
    output(tiles - 1, weights)


def gradient_tiles(q_ref, c_ref, v_ref, kft, state, grad, before, first_tile, tiles):
    heads = grad.shape[0]
    ahead = later_key(heads)
    group = 2 if tiles % 2 == 0 else 1
    now = state[...]
    starts, turned, backs, found, q = {}, {}, {}, {}, {}

    def load(t, now):
        if t >= tiles:
            return now
        here = at_tile(first_tile + t)
        turned[t] = below(head_rows(c_ref, first_tile + t, heads)).T
        q[t] = head_rows(q_ref, first_tile + t, heads)
        starts[t] = now.astype(BF16)
        return now + nn(kft[:, here], v_ref[here, :])

    def score(t):
        if t < tiles:
            back = nn(v_ref[at_tile(first_tile + t), :], turned[t])
            backs[t] = jnp.where(ahead, 0.0, back).astype(BF16)

    def gradient(t):
        left = beside([kft[:, at_tile(first_tile + t)], starts[t]])
        out = nn(left, below([backs[t], turned[t]])) * scale_of(before, first_tile + t, heads)
        found[t] = columns(out.astype(BF16))

    def add(ts):
        for h in range(heads):
            grad[h] += nn(beside([found[t][h] for t in ts]), below([q[t][h] for t in ts]))

    now = load(1, load(0, now))
    score(0)
    for t in range(tiles):
        now = load(t + 2, now)
        score(t + 1)
        gradient(t)
        if t and t % group == 0:
            add(range(t - group, t))
    add(range(tiles - group, tiles))
    state[...] = now


def linear_tiles(q_ref, kf_ref, vt_ref, maps_t, state, out_ref, first_token):
    heads, hd = q_ref.shape[1:]
    tiles = q_ref.shape[0] // TILE
    ahead = later_key(heads)
    group = 2 if tiles % 2 == 0 else 1
    q = pltpu.einshape("tha->hta", q_ref[...])
    now = state[...]
    starts, turned, inside, done = {}, {}, {}, []

    def load(t, now):
        if t >= tiles:
            return now
        if t % group == 0:
            rows = slice(t * TILE, (t + group) * TILE)
            features = [columns(nt(maps_t[h], q[h, rows]).astype(BF16)) for h in range(heads)]
            for i in range(group):
                turned[t + i] = beside([f[i] for f in features])
        starts[t] = now.astype(BF16)
        return now + nn(vt_ref[t, :hd], kf_ref[at_tile(t), :])

    def score(t):
        if t < tiles:
            scores = nn(kf_ref[at_tile(t), :], turned[t])
            inside[t] = jnp.where(ahead, 0.0, scores).astype(BF16)

    def output(t):
        left = beside([vt_ref[t, :hd], starts[t]])
        out = nn(left, below([inside[t], turned[t]])) * scale_of(first_token, t, heads)
        done.append([x.T for x in columns(out.astype(BF16))])

    now = load(1, load(0, now))
    score(0)
    for t in range(tiles):
        now = load(t + 2, now)
        score(t + 1)
        output(t)
    state[...] = now
    out_ref[...] = pltpu.einshape("hta->tha", below([below([d[h] for d in done])[None] for h in range(heads)]))


def first_kernel(
    count, step_tiles,
    q_hbm, c_hbm, k_hbm, v_hbm, key_map_ref,
    soft_hbm, kf_hbm, vt_hbm, prefix_ref, mine_ref,
    q_all, c_all, k_ext, v_all, v_ext, kf, kft, soft_all,
    local_sum, sums, halo, state, grad, pieces, pieces16, slots,
    load_sem, store_sem, sum_send, sum_recv, halo_send, halo_recv, piece_send, piece_recv,
):
    rank = lax.axis_index("seq")
    heads, hd = grad.shape[:2]
    tokens_here = v_all.shape[0]
    blocks = tokens_here // TILE
    share = hd // count
    half = blocks // 2
    before = rank * tokens_here

    def halo_copy(i):
        return pltpu.make_async_remote_copy(
            src_ref=(k_ext.at[pl.ds(tokens_here, W)], v_all.at[pl.ds(tokens_here - W, W)])[i],
            dst_ref=halo.at[i],
            send_sem=halo_send.at[i],
            recv_sem=halo_recv.at[i],
            device_id={"seq": rank + 1},
            device_id_type=MESH,
        )

    def sum_copy(k):
        return pltpu.make_async_remote_copy(
            src_ref=local_sum,
            dst_ref=sums.at[k - 1],
            send_sem=sum_send.at[k - 1],
            recv_sem=sum_recv.at[k - 1],
            device_id={"seq": rank + k},
            device_id_type=MESH,
        )

    def piece_copy(k):
        target = lax.rem(rank + k, count)
        return pltpu.make_async_remote_copy(
            src_ref=pieces16.at[target],
            dst_ref=slots.at[k - 1],
            send_sem=piece_send.at[k - 1],
            recv_sem=piece_recv.at[k - 1],
            device_id={"seq": target},
            device_id_type=MESH,
        )

    rows = TILE * heads
    late, soon = pl.ds(half * rows, (blocks - half) * rows), pl.ds(0, half * rows)
    loads = [
        pltpu.make_async_copy(source, target, load_sem.at[i])
        for i, (source, target) in enumerate([
            (k_hbm, k_ext.at[pl.ds(W, tokens_here)]),
            (v_hbm, v_all),
            (q_hbm.at[late], q_all.at[late]),
            (c_hbm, c_all),
            (q_hbm.at[soon], q_all.at[soon]),
        ])
    ]
    barrier = pltpu.get_barrier_semaphore()
    for k in range(1, count):
        pl.semaphore_signal(barrier, inc=1, device_id={"seq": lax.rem(rank + k, count)}, device_id_type=MESH)
    for load in loads[:3]:
        load.start()
    loads[0].wait()
    key_map_t = key_map_ref[...].astype(F32).T.astype(BF16)
    kft[...] = nt(key_map_t, k_ext[W:]).astype(BF16)
    kf[...] = nn(k_ext[W:], key_map_ref[...]).astype(BF16)
    loads[1].wait()
    local_sum[...] = nn(kft[...], v_all[...]).astype(BF16)
    for b in range(blocks):
        v_ext[MIDS + b, :hd] = v_all[b * TILE : (b + 1) * TILE, :].T
    v_ext[MIDS:, hd:] = jnp.ones((blocks, ONES, TILE), BF16)
    grad[...] = jnp.zeros_like(grad)
    state[...] = jnp.zeros_like(state)
    for load in loads[3:]:
        load.start()
    stores = [
        pltpu.make_async_copy(kf, kf_hbm, store_sem.at[0]),
        pltpu.make_async_copy(v_ext.at[pl.ds(MIDS, blocks)], vt_hbm, store_sem.at[1]),
        pltpu.make_async_copy(soft_all.at[late], soft_hbm.at[late], store_sem.at[2]),
        pltpu.make_async_copy(soft_all.at[soon], soft_hbm.at[soon], store_sem.at[3]),
    ]
    stores[0].start()
    stores[1].start()
    loads[2].wait()

    def softmax(first_tile, tiles):
        softmax_tiles(q_all, k_ext, v_ext, soft_all, first_tile, tiles, heads)

    lead = step_tiles // 2
    softmax(half, lead)

    pl.semaphore_wait(barrier, count - 1)
    for k in range(1, count):
        @pl.when(rank + k < count)
        def _():
            sum_copy(k).start()
    @pl.when(rank + 1 < count)
    def _():
        halo_copy(0).start()
        halo_copy(1).start()

    rest = (half - lead) // 2
    @pl.loop(0, 2)
    def _(i):
        softmax(half + lead + i * rest, rest)

    stores[2].start()
    for k in range(1, count):
        @pl.when(rank + k < count)
        def _():
            sum_copy(k).wait_send()
        @pl.when(rank >= k)
        def _():
            sum_copy(k).wait_recv()
            state[...] += sums[k - 1].astype(F32)
    prefix_ref[...] = state[...].T
    loads[3].wait()
    loads[4].wait()

    @pl.loop(0, blocks // step_tiles)
    def _(i):
        gradient_tiles(q_all, c_all, v_all, kft, state, grad, before, i * step_tiles, step_tiles)

    for h in range(heads):
        turned = grad[h].T
        for p in range(count):
            piece = turned[p * share : (p + 1) * share]
            pieces[p, :, h * hd : (h + 1) * hd] = piece
            pieces16[p, :, h * hd : (h + 1) * hd] = piece.astype(BF16)
    for k in range(1, count):
        piece_copy(k).start()

    @pl.loop(0, half // step_tiles)
    def _(i):
        @pl.when(i == half // step_tiles - 1)
        def _():
            @pl.when(rank + 1 < count)
            def _():
                halo_copy(0).wait_send()
                halo_copy(1).wait_send()
            @pl.when(rank >= 1)
            def _():
                halo_copy(0).wait_recv()
                halo_copy(1).wait_recv()
                k_ext[:W] = halo[0]
                for b in range(MIDS):
                    v_ext[b, :hd] = halo[1, b * TILE : (b + 1) * TILE, :].T
                    v_ext[b, hd:] = jnp.ones((ONES, TILE), BF16)
            @pl.when(rank == 0)
            def _():
                k_ext[:W] = jnp.broadcast_to(k_ext[W : W + 1, :], (W, hd))
                v_ext[:MIDS] = jnp.zeros((MIDS,) + v_ext.shape[1:], BF16)
        softmax(half - (i + 1) * step_tiles, step_tiles)

    stores[3].start()
    total = pieces[rank]
    for k in range(1, count):
        piece_copy(k).wait()
        total = total + slots[k - 1].astype(F32)
    mine_ref[...] = total
    for store in stores:
        store.wait()


def last_kernel(
    steps,
    q_ref, kf_ref, vt_ref, soft_in_hbm, maps_ref, prefix_ref, mine_in_ref,
    linear_ref, soft_hbm, mine_ref,
    soft_all, maps_t, state, load_sem, store_sem,
):
    step = pl.program_id(0)
    heads, hd = q_ref.shape[1:]
    step_tokens = q_ref.shape[0]
    rows = step_tokens * heads

    def part(i):
        return pl.ds(pl.multiple_of(i * rows, rows), rows)

    def load(i):
        return pltpu.make_async_copy(soft_in_hbm.at[part(i)], soft_all.at[part(i)], load_sem.at[i])

    def store(i):
        return pltpu.make_async_copy(soft_all.at[part(i)], soft_hbm.at[part(i)], store_sem.at[i])

    @pl.when(step == 0)
    def _():
        for i in range(steps):
            load(i).start()
        for h in range(heads):
            maps_t[h] = maps_ref[h].T
            mine_ref[:, h, :] = mine_in_ref[:, h * hd : (h + 1) * hd]
        state[...] = prefix_ref[...]

    @pl.when(step >= 1)
    def _():
        load(step - 1).wait()
        store(step - 1).start()

    @pl.when(step == steps - 1)
    def _():
        load(step).wait()
        store(step).start()

    first_token = (lax.axis_index("seq") * steps + step) * step_tokens
    linear_tiles(q_ref, kf_ref, vt_ref, maps_t, state, linear_ref, first_token)

    @pl.when(step == steps - 1)
    def _():
        for i in range(steps):
            store(i).wait()


def per_device(queries, keys, values, query_maps, key_map, linear_cotangent):
    tokens_here, hd = keys.shape
    heads = queries.shape[1]
    count = lax.axis_size("seq")
    share = hd // count
    blocks = tokens_here // TILE
    step_tiles = 8
    steps = blocks // step_tiles
    flat = (tokens_here * heads, hd)
    dma = pltpu.SemaphoreType.DMA
    hbm = pl.BlockSpec(memory_space=pl.ANY)
    vmem = pl.BlockSpec(memory_space=pltpu.VMEM)

    rows16 = jax.ShapeDtypeStruct(flat, BF16)
    kf16 = jax.ShapeDtypeStruct((tokens_here, hd), BF16)
    vt16 = jax.ShapeDtypeStruct((blocks, hd + ONES, TILE), BF16)
    square = jax.ShapeDtypeStruct((hd, hd), F32)
    piece = jax.ShapeDtypeStruct((share, heads * hd), F32)
    soft, key_features, values_t, prefix, mine = pl.pallas_call(
        functools.partial(first_kernel, count, step_tiles),
        in_specs=[hbm, hbm, hbm, hbm, vmem],
        out_specs=[hbm, hbm, hbm, vmem, vmem],
        out_shape=[rows16, kf16, vt16, square, piece],
        scratch_shapes=[
            pltpu.VMEM(flat, BF16),
            pltpu.VMEM(flat, BF16),
            pltpu.VMEM((tokens_here + W, hd), BF16),
            pltpu.VMEM((tokens_here, hd), BF16),
            pltpu.VMEM((blocks + MIDS, hd + ONES, TILE), BF16),
            pltpu.VMEM((tokens_here, hd), BF16),
            pltpu.VMEM((hd, tokens_here), BF16),
            pltpu.VMEM(flat, BF16),
            pltpu.VMEM((hd, hd), BF16),
            pltpu.VMEM((count - 1, hd, hd), BF16),
            pltpu.VMEM((2, W, hd), BF16),
            pltpu.VMEM((hd, hd), F32),
            pltpu.VMEM((heads, hd, hd), F32),
            pltpu.VMEM((count, share, heads * hd), F32),
            pltpu.VMEM((count, share, heads * hd), BF16),
            pltpu.VMEM((count - 1, share, heads * hd), BF16),
            dma((5,)), dma((4,)),
            dma((count - 1,)), dma((count - 1,)), dma((2,)), dma((2,)), dma((count - 1,)), dma((count - 1,)),
        ],
        compiler_params=pltpu.CompilerParams(collective_id=0, has_side_effects=True),
        name="softmax_and_gradient",
    )(queries.reshape(flat), linear_cotangent.reshape(flat), keys, values, key_map)

    once = lambda a: pl.BlockSpec(a.shape, lambda i: (0,) * len(a.shape), pipeline_mode=pl.Buffered(1))
    tokens = step_tiles * TILE
    along = pl.BlockSpec((tokens, heads, hd), lambda i: (i, 0, 0))
    final = jax.ShapeDtypeStruct((share, heads, hd), F32)
    linear, soft, mine = pl.pallas_call(
        functools.partial(last_kernel, steps),
        grid=(steps,),
        in_specs=[
            along,
            pl.BlockSpec((tokens, hd), lambda i: (i, 0)),
            pl.BlockSpec((step_tiles, hd + ONES, TILE), lambda i: (i, 0, 0)),
            hbm, once(query_maps), once(prefix), once(mine),
        ],
        out_specs=[along, hbm, once(final)],
        out_shape=[jax.ShapeDtypeStruct((tokens_here, heads, hd), BF16), rows16, final],
        scratch_shapes=[
            pltpu.VMEM(flat, BF16),
            pltpu.VMEM((heads, hd, hd), BF16),
            pltpu.VMEM((hd, hd), F32),
            dma((steps,)), dma((steps,)),
        ],
        compiler_params=pltpu.CompilerParams(dimension_semantics=("arbitrary",)),
        name="linear",
    )(queries, key_features, values_t, soft, query_maps, prefix, mine)
    return soft.reshape(queries.shape), linear, mine


def solution(mesh):
    rows = P(("groups", "seq"), ("head", "rep"), None)
    return jax.shard_map(
        per_device,
        mesh=mesh,
        in_specs=(
            rows,
            P(("groups", "seq"), None),
            P(("groups", "seq"), None),
            P(("groups", "head", "rep"), None, None),
            P("groups", None),
            rows,
        ),
        out_specs=(rows, rows, rows),
        check_vma=False,
    )
```

```python
import functools

import jax
import jax.numpy as jnp
from jax import lax
from jax.experimental import pallas as pl
from jax.experimental.pallas import tpu as pltpu
from jax.sharding import PartitionSpec as P

W = 512
TILE = 128
MIDS = W // TILE
ONES = 16
MESH = pl.DeviceIdType.MESH
F32 = jnp.float32
BF16 = jnp.bfloat16


def nt(a, b):
    return lax.dot_general(a, b, (((1,), (1,)), ((), ())), preferred_element_type=F32)


def nn(a, b):
    return jnp.dot(a, b, preferred_element_type=F32)


def beside(parts):
    return parts[0] if len(parts) == 1 else jnp.concatenate(parts, 1)


def below(parts):
    return parts[0] if len(parts) == 1 else jnp.concatenate(parts, 0)


def later_key(heads):
    shape = (TILE, TILE)
    one = lax.broadcasted_iota(jnp.int32, shape, 0) > lax.broadcasted_iota(jnp.int32, shape, 1)
    return beside([one] * heads)


def later_key_in_band(heads):
    shape = (TILE // heads, TILE)
    return lax.broadcasted_iota(jnp.int32, shape, 0) > lax.broadcasted_iota(jnp.int32, shape, 1) // heads


def columns(x):
    return [x[:, h : h + TILE] for h in range(0, x.shape[1], TILE)]


def at_tile(tile, rows=TILE):
    return pl.ds(pl.multiple_of(tile * rows, rows), rows)


def head_rows(ref, tile, heads):
    if heads == 1:
        return [ref[at_tile(tile), :]]
    own = ref.at[at_tile(tile, TILE * heads), :]
    return [own[pl.ds(h, TILE, stride=heads), :] for h in range(heads)]


def scale_of(before, tile, heads):
    token = lax.broadcasted_iota(jnp.int32, (1, TILE), 1) + (before + tile * TILE + 1)
    return beside([lax.rsqrt(token.astype(F32))] * heads)


def softmax_weights(scores, heads, hd):
    scale = hd ** (-0.5) * 1.4426950408889634
    ahead = later_key_in_band(heads)
    span = TILE // heads
    found = []
    for part, chunk in enumerate(scores):
        skipped = part * (chunk.shape[0] - W)
        for i, own in enumerate(columns(chunk)):
            a = skipped + i * span
            b = a + span
            rows = lambda start, stop: own[start - skipped : stop - skipped]
            edge = [rows(W, W + a)] * (a > 0) + [jnp.where(ahead, rows(a, b), rows(W + a, W + b))]
            edge = below(edge + [rows(b, TILE)] * (b < TILE))
            kept = [edge] + [rows(j * TILE, (j + 1) * TILE) for j in range(1, MIDS)]
            highest = jnp.max(functools.reduce(jnp.maximum, kept), axis=0, keepdims=True)
            kept = [jnp.exp2((p - highest) * scale) for p in kept]
            edge = kept[0]
            old = [jnp.zeros((a, TILE), BF16)] * (a > 0) + [jnp.where(ahead, edge[a:b], 0.0).astype(BF16)]
            new = [jnp.where(ahead, 0.0, edge[a:b]).astype(BF16)]
            if a > 0:
                new = [edge[:a].astype(BF16)] + new
            if b < TILE:
                old = old + [edge[b:].astype(BF16)]
                new = new + [jnp.zeros((TILE - b, TILE), BF16)]
            total = jnp.sum(functools.reduce(jnp.add, kept), axis=0, keepdims=True)
            found.append((below(old + [p.astype(BF16) for p in kept[1:]] + new), total))
    return beside([f[0] for f in found]), beside([f[1] for f in found])


def softmax_tiles(q_ref, k_ext, v_ext, out_ref, first_tile, tiles, heads, present, meanwhile, stored):
    hd = q_ref.shape[1]
    rows = TILE * heads
    lanes = min(2 * TILE, rows)
    span = lanes // heads

    def scores(t):
        found = []
        for i in range(rows // lanes):
            keys = k_ext[pl.ds(pl.multiple_of((first_tile + t) * TILE + i * span, span), W + span), :]
            queries = q_ref[pl.ds(pl.multiple_of((first_tile + t) * rows + i * lanes, lanes), lanes), :]
            found.append(nt(keys, queries))
        return found

    def output(t, found):
        weights, total = found
        values = beside([v_ext[first_tile + t + j] for j in range(MIDS + 1)])
        if present is not None and t < MIDS:
            ones = jnp.ones((ONES, TILE), BF16)
            values = below([values, beside([present if t + j < MIDS else ones for j in range(MIDS + 1)])])
        out = nn(values, weights)
        if present is not None and t < MIDS:
            total = out[hd : hd + 1]
        out_ref[at_tile(first_tile + t, rows), :] = (out[:hd] * (1.0 / total)).astype(BF16).T
        stored(t)

    weights, now = None, scores(0)
    if meanwhile is not None:
        meanwhile()
    for t in range(tiles):
        after = scores(t + 1) if t + 1 < tiles else None
        fresh = softmax_weights(now, heads, hd)
        if weights is not None:
            output(t - 1, weights)
        now, weights = after, fresh
    output(tiles - 1, weights)


def gradient_tiles(q_ref, c_ref, v_ref, kft, state, grad, before, first_tile, tiles):
    heads = grad.shape[0]
    ahead = later_key(heads)
    group = 2 if tiles % 2 == 0 else 1
    now = state[...]
    starts, turned, backs, found, q = {}, {}, {}, {}, {}

    def load(t, now):
        if t >= tiles:
            return now
        here = at_tile(first_tile + t)
        turned[t] = below(head_rows(c_ref, first_tile + t, heads)).T
        q[t] = head_rows(q_ref, first_tile + t, heads)
        starts[t] = now.astype(BF16)
        return now + nn(kft[:, here], v_ref[here, :])

    def score(t):
        if t < tiles:
            back = nn(v_ref[at_tile(first_tile + t), :], turned[t])
            backs[t] = jnp.where(ahead, 0.0, back).astype(BF16)

    def gradient(t):
        left = beside([kft[:, at_tile(first_tile + t)], starts[t]])
        out = nn(left, below([backs[t], turned[t]])) * scale_of(before, first_tile + t, heads)
        found[t] = columns(out.astype(BF16))

    def add(ts):
        for h in range(heads):
            grad[h] += nn(beside([found[t][h] for t in ts]), below([q[t][h] for t in ts]))

    now = load(1, load(0, now))
    score(0)
    for t in range(tiles):
        now = load(t + 2, now)
        score(t + 1)
        gradient(t)
        if t and t % group == 0:
            add(range(t - group, t))
    add(range(tiles - group, tiles))
    state[...] = now


def linear_tiles(q_ref, kf_ref, vt_ref, maps_t, state, out_ref, first_token):
    heads, hd = q_ref.shape[1:]
    tiles = q_ref.shape[0] // TILE
    ahead = later_key(heads)
    group = 2 if tiles % 2 == 0 else 1
    q = pltpu.einshape("tha->hta", q_ref[...])
    now = state[...]
    starts, turned, inside, done = {}, {}, {}, []

    def load(t, now):
        if t >= tiles:
            return now
        if t % group == 0:
            rows = slice(t * TILE, (t + group) * TILE)
            features = [columns(nt(maps_t[h], q[h, rows]).astype(BF16)) for h in range(heads)]
            for i in range(group):
                turned[t + i] = beside([f[i] for f in features])
        starts[t] = now.astype(BF16)
        return now + nn(vt_ref[t], kf_ref[at_tile(t), :])

    def score(t):
        if t < tiles:
            scores = nn(kf_ref[at_tile(t), :], turned[t])
            inside[t] = jnp.where(ahead, 0.0, scores).astype(BF16)

    def output(t):
        left = beside([vt_ref[t], starts[t]])
        out = nn(left, below([inside[t], turned[t]])) * scale_of(first_token, t, heads)
        done.append([x.T for x in columns(out.astype(BF16))])

    now = load(1, load(0, now))
    score(0)
    for t in range(tiles):
        now = load(t + 2, now)
        score(t + 1)
        output(t)
    state[...] = now
    out_ref[...] = pltpu.einshape("hta->tha", below([below([d[h] for d in done])[None] for h in range(heads)]))


def first_kernel(
    count, step_tiles,
    q_hbm, c_hbm, k_hbm, v_hbm, key_map_ref,
    soft_hbm, vt_hbm, prefix_ref, mine_ref,
    q_all, c_all, k_ext, v_all, v_ext, kft, soft_all,
    local_sum, sums, halo, state, grad, pieces, pieces16, slots,
    load_sem, store_sem, sum_send, sum_recv, halo_send, halo_recv, piece_send, piece_recv,
):
    rank = lax.axis_index("seq")
    heads, hd = grad.shape[:2]
    tokens_here = v_all.shape[0]
    blocks = tokens_here // TILE
    share = hd // count
    half = blocks // 2
    before = rank * tokens_here

    def halo_copy(i):
        return pltpu.make_async_remote_copy(
            src_ref=(k_ext.at[pl.ds(tokens_here, W)], v_all.at[pl.ds(tokens_here - W, W)])[i],
            dst_ref=halo.at[i],
            send_sem=halo_send.at[i],
            recv_sem=halo_recv.at[i],
            device_id={"seq": rank + 1},
            device_id_type=MESH,
        )

    def sum_copy(k):
        return pltpu.make_async_remote_copy(
            src_ref=local_sum,
            dst_ref=sums.at[k - 1],
            send_sem=sum_send.at[k - 1],
            recv_sem=sum_recv.at[k - 1],
            device_id={"seq": rank + k},
            device_id_type=MESH,
        )

    def piece_copy(k):
        target = lax.rem(rank + k, count)
        return pltpu.make_async_remote_copy(
            src_ref=pieces16.at[target],
            dst_ref=slots.at[k - 1],
            send_sem=piece_send.at[k - 1],
            recv_sem=piece_recv.at[k - 1],
            device_id={"seq": target},
            device_id_type=MESH,
        )

    rows = TILE * heads
    lead = step_tiles // 2

    def tiles_of(first, tiles):
        return pl.ds(first * rows, tiles * rows)

    first_part, late, soon = tiles_of(half, lead), tiles_of(half + lead, blocks - half - lead), tiles_of(0, half)
    loads = [
        pltpu.make_async_copy(source, target, load_sem.at[i])
        for i, (source, target) in enumerate([
            (k_hbm, k_ext.at[pl.ds(W, tokens_here)]),
            (v_hbm, v_all),
            (q_hbm.at[first_part], q_all.at[first_part]),
            (q_hbm.at[late], q_all.at[late]),
            (c_hbm, c_all),
            (q_hbm.at[soon], q_all.at[soon]),
        ])
    ]

    def soft_store(i):
        part = tiles_of(i * lead, lead)
        return pltpu.make_async_copy(soft_all.at[part], soft_hbm.at[part], store_sem.at[i])

    def softmax(first_tile, tiles, present=None, meanwhile=None):
        def stored(t):
            if (t + 1) % lead == 0:
                soft_store((first_tile + t) // lead).start()

        softmax_tiles(q_all, k_ext, v_ext, soft_all, first_tile, tiles, heads, present, meanwhile, stored)

    barrier = pltpu.get_barrier_semaphore()
    for k in range(1, count):
        pl.semaphore_signal(barrier, inc=1, device_id={"seq": lax.rem(rank + k, count)}, device_id_type=MESH)
    for load in loads[:3]:
        load.start()
    grad[...] = jnp.zeros_like(grad)
    state[...] = jnp.zeros_like(state)
    for load in loads[3:]:
        load.start()
    key_map_t = key_map_ref[...].astype(F32).T.astype(BF16)
    loads[0].wait()
    kft[...] = nt(key_map_t, k_ext[W:]).astype(BF16)
    loads[1].wait()
    loads[2].wait()
    for b in range(blocks):
        v_ext[MIDS + b] = v_all[b * TILE : (b + 1) * TILE, :].T

    def shard_sum():
        near, far = slice(0, tokens_here // 2), slice(tokens_here // 2, tokens_here)
        local_sum[...] = (nn(kft[:, near], v_all[near, :]) + nn(kft[:, far], v_all[far, :])).astype(BF16)

    softmax(half, lead, meanwhile=shard_sum)
    vt_store = pltpu.make_async_copy(v_ext.at[pl.ds(MIDS, blocks)], vt_hbm, store_sem.at[blocks // lead])
    vt_store.start()

    pl.semaphore_wait(barrier, count - 1)
    for k in range(1, count):
        @pl.when(rank + k < count)
        def _():
            sum_copy(k).start()
    @pl.when(rank + 1 < count)
    def _():
        halo_copy(0).start()
        halo_copy(1).start()

    loads[3].wait()
    softmax(half + lead, blocks - half - lead)

    for k in range(1, count):
        @pl.when(rank + k < count)
        def _():
            sum_copy(k).wait_send()
        @pl.when(rank >= k)
        def _():
            sum_copy(k).wait_recv()
            state[...] += sums[k - 1].astype(F32)
    prefix_ref[...] = state[...].T
    loads[4].wait()
    loads[5].wait()

    @pl.loop(0, blocks // (2 * step_tiles))
    def _(i):
        gradient_tiles(q_all, c_all, v_all, kft, state, grad, before, i * 2 * step_tiles, 2 * step_tiles)

    for h in range(heads):
        turned = grad[h].T
        for p in range(count):
            piece = turned[p * share : (p + 1) * share]
            pieces[p, :, h * hd : (h + 1) * hd] = piece
            pieces16[p, :, h * hd : (h + 1) * hd] = piece.astype(BF16)
    for k in range(1, count):
        piece_copy(k).start()

    @pl.when(rank + 1 < count)
    def _():
        halo_copy(0).wait_send()
        halo_copy(1).wait_send()
    @pl.when(rank >= 1)
    def _():
        halo_copy(0).wait_recv()
        halo_copy(1).wait_recv()
        k_ext[:W] = halo[0]
        for b in range(MIDS):
            v_ext[b] = halo[1, b * TILE : (b + 1) * TILE, :].T
    @pl.when(rank == 0)
    def _():
        k_ext[:W] = jnp.broadcast_to(k_ext[W : W + 1, :], (W, hd))
        v_ext[:MIDS] = jnp.zeros((MIDS,) + v_ext.shape[1:], BF16)
    softmax(0, half, jnp.where(rank == 0, jnp.zeros((ONES, TILE), F32), 1.0).astype(BF16))

    total = pieces[rank]
    for k in range(1, count):
        piece_copy(k).wait()
        total = total + slots[k - 1].astype(F32)
    mine_ref[...] = total
    for i in range(blocks // lead):
        soft_store(i).wait()
    vt_store.wait()


def last_kernel(
    steps,
    q_ref, k_first_ref, k_next_ref, vt_ref, soft_in_hbm, key_map_ref, maps_ref, prefix_ref, mine_in_ref,
    linear_ref, soft_hbm, mine_ref,
    kf, soft_all, maps_t, state, load_sem, store_sem,
):
    step = pl.program_id(0)
    heads, hd = q_ref.shape[1:]
    step_tokens = q_ref.shape[0]
    rows = step_tokens * heads

    def part(i):
        return pl.ds(pl.multiple_of(i * rows, rows), rows)

    def load(i):
        return pltpu.make_async_copy(soft_in_hbm.at[part(i)], soft_all.at[part(i)], load_sem.at[i])

    def store(i):
        return pltpu.make_async_copy(soft_all.at[part(i)], soft_hbm.at[part(i)], store_sem.at[i])

    @pl.when(step == 0)
    def _():
        for i in range(steps):
            load(i).start()
        kf[0] = nn(k_first_ref[...], key_map_ref[...]).astype(BF16)
        for h in range(heads):
            maps_t[h] = maps_ref[h].T
            mine_ref[:, h, :] = mine_in_ref[:, h * hd : (h + 1) * hd]
        state[...] = prefix_ref[...]

    @pl.when(step >= 1)
    def _():
        load(step - 1).wait()
        store(step - 1).start()

    @pl.when(step == steps - 1)
    def _():
        load(step).wait()
        store(step).start()

    first_token = (lax.axis_index("seq") * steps + step) * step_tokens
    linear_tiles(q_ref, kf.at[lax.rem(step, 2)], vt_ref, maps_t, state, linear_ref, first_token)
    kf[lax.rem(step + 1, 2)] = nn(k_next_ref[...], key_map_ref[...]).astype(BF16)

    @pl.when(step == steps - 1)
    def _():
        for i in range(steps):
            store(i).wait()


def per_device(queries, keys, values, query_maps, key_map, linear_cotangent):
    tokens_here, hd = keys.shape
    heads = queries.shape[1]
    count = lax.axis_size("seq")
    share = hd // count
    blocks = tokens_here // TILE
    step_tiles = 8
    steps = blocks // step_tiles
    flat = (tokens_here * heads, hd)
    dma = pltpu.SemaphoreType.DMA
    hbm = pl.BlockSpec(memory_space=pl.ANY)
    vmem = pl.BlockSpec(memory_space=pltpu.VMEM)

    rows16 = jax.ShapeDtypeStruct(flat, BF16)
    vt16 = jax.ShapeDtypeStruct((blocks, hd, TILE), BF16)
    square = jax.ShapeDtypeStruct((hd, hd), F32)
    piece = jax.ShapeDtypeStruct((share, heads * hd), F32)
    soft, values_t, prefix, mine = pl.pallas_call(
        functools.partial(first_kernel, count, step_tiles),
        in_specs=[hbm, hbm, hbm, hbm, vmem],
        out_specs=[hbm, hbm, vmem, vmem],
        out_shape=[rows16, vt16, square, piece],
        scratch_shapes=[
            pltpu.VMEM(flat, BF16),
            pltpu.VMEM(flat, BF16),
            pltpu.VMEM((tokens_here + W, hd), BF16),
            pltpu.VMEM((tokens_here, hd), BF16),
            pltpu.VMEM((blocks + MIDS, hd, TILE), BF16),
            pltpu.VMEM((hd, tokens_here), BF16),
            pltpu.VMEM(flat, BF16),
            pltpu.VMEM((hd, hd), BF16),
            pltpu.VMEM((count - 1, hd, hd), BF16),
            pltpu.VMEM((2, W, hd), BF16),
            pltpu.VMEM((hd, hd), F32),
            pltpu.VMEM((heads, hd, hd), F32),
            pltpu.VMEM((count, share, heads * hd), F32),
            pltpu.VMEM((count, share, heads * hd), BF16),
            pltpu.VMEM((count - 1, share, heads * hd), BF16),
            dma((6,)), dma((blocks // (step_tiles // 2) + 1,)),
            dma((count - 1,)), dma((count - 1,)), dma((2,)), dma((2,)), dma((count - 1,)), dma((count - 1,)),
        ],
        compiler_params=pltpu.CompilerParams(collective_id=0, has_side_effects=True),
        name="softmax_and_gradient",
    )(queries.reshape(flat), linear_cotangent.reshape(flat), keys, values, key_map)

    once = lambda a: pl.BlockSpec(a.shape, lambda i: (0,) * len(a.shape), pipeline_mode=pl.Buffered(1))
    tokens = step_tiles * TILE
    along = pl.BlockSpec((tokens, heads, hd), lambda i: (i, 0, 0))
    final = jax.ShapeDtypeStruct((share, heads, hd), F32)
    linear, soft, mine = pl.pallas_call(
        functools.partial(last_kernel, steps),
        grid=(steps,),
        in_specs=[
            along,
            pl.BlockSpec((tokens, hd), lambda i: (0, 0), pipeline_mode=pl.Buffered(1)),
            pl.BlockSpec((tokens, hd), lambda i: (jnp.minimum(i + 1, steps - 1), 0)),
            pl.BlockSpec((step_tiles, hd, TILE), lambda i: (i, 0, 0)),
            hbm, once(key_map), once(query_maps), once(prefix), once(mine),
        ],
        out_specs=[along, hbm, once(final)],
        out_shape=[jax.ShapeDtypeStruct((tokens_here, heads, hd), BF16), rows16, final],
        scratch_shapes=[
            pltpu.VMEM((2, tokens, hd), BF16),
            pltpu.VMEM(flat, BF16),
            pltpu.VMEM((heads, hd, hd), BF16),
            pltpu.VMEM((hd, hd), F32),
            dma((steps,)), dma((steps,)),
        ],
        compiler_params=pltpu.CompilerParams(dimension_semantics=("arbitrary",)),
        name="linear",
    )(queries, keys, keys, values_t, soft, key_map, query_maps, prefix, mine)
    return soft.reshape(queries.shape), linear, mine


def solution(mesh):
    rows = P(("groups", "seq"), ("head", "rep"), None)
    return jax.shard_map(
        per_device,
        mesh=mesh,
        in_specs=(
            rows,
            P(("groups", "seq"), None),
            P(("groups", "seq"), None),
            P(("groups", "head", "rep"), None, None),
            P("groups", None),
            rows,
        ),
        out_specs=(rows, rows, rows),
        check_vma=False,
    )
```

```python
import functools

import jax
import jax.numpy as jnp
from jax import lax
from jax.experimental import pallas as pl
from jax.experimental.pallas import tpu as pltpu
from jax.sharding import PartitionSpec as P

W = 512
TILE = 128
MIDS = W // TILE
ONES = 16
LAG = 3
DEPTH = 2
LATE = 1
MESH = pl.DeviceIdType.MESH
F32 = jnp.float32
BF16 = jnp.bfloat16


def nt(a, b):
    return lax.dot_general(a, b, (((1,), (1,)), ((), ())), preferred_element_type=F32)


def nn(a, b):
    return jnp.dot(a, b, preferred_element_type=F32)


def beside(parts):
    return parts[0] if len(parts) == 1 else jnp.concatenate(parts, 1)


def below(parts):
    return parts[0] if len(parts) == 1 else jnp.concatenate(parts, 0)


def later_key(heads):
    shape = (TILE, TILE)
    one = lax.broadcasted_iota(jnp.int32, shape, 0) > lax.broadcasted_iota(jnp.int32, shape, 1)
    return beside([one] * heads)


def later_key_in_band(heads):
    shape = (TILE // heads, TILE)
    return lax.broadcasted_iota(jnp.int32, shape, 0) > lax.broadcasted_iota(jnp.int32, shape, 1) // heads


def columns(x):
    return [x[:, h : h + TILE] for h in range(0, x.shape[1], TILE)]


def at_tile(tile, rows=TILE):
    return pl.ds(pl.multiple_of(tile * rows, rows), rows)


def head_rows(ref, tile, heads):
    if heads == 1:
        return [ref[at_tile(tile), :]]
    own = ref.at[at_tile(tile, TILE * heads), :]
    return [own[pl.ds(h, TILE, stride=heads), :] for h in range(heads)]


def scale_of(before, tile, heads):
    token = lax.broadcasted_iota(jnp.int32, (1, TILE), 1) + (before + tile * TILE + 1)
    return beside([lax.rsqrt(token.astype(F32))] * heads)


def softmax_weights(chunk, part, heads, hd):
    scale = hd ** (-0.5) * 1.4426950408889634
    ahead = later_key_in_band(heads)
    span = TILE // heads
    skipped = part * (chunk.shape[0] - W)
    found = []
    for i, own in enumerate(columns(chunk)):
        a = skipped + i * span
        b = a + span
        rows = lambda start, stop: own[start - skipped : stop - skipped]
        edge = [rows(W, W + a)] * (a > 0) + [jnp.where(ahead, rows(a, b), rows(W + a, W + b))]
        edge = below(edge + [rows(b, TILE)] * (b < TILE))
        kept = [edge] + [rows(j * TILE, (j + 1) * TILE) for j in range(1, MIDS)]
        highest = jnp.max(functools.reduce(jnp.maximum, kept), axis=0, keepdims=True)
        kept = [jnp.exp2((p - highest) * scale) for p in kept]
        edge = kept[0]
        old = [jnp.zeros((a, TILE), BF16)] * (a > 0) + [jnp.where(ahead, edge[a:b], 0.0).astype(BF16)]
        new = [jnp.where(ahead, 0.0, edge[a:b]).astype(BF16)]
        if a > 0:
            new = [edge[:a].astype(BF16)] + new
        if b < TILE:
            old = old + [edge[b:].astype(BF16)]
            new = new + [jnp.zeros((TILE - b, TILE), BF16)]
        total = jnp.sum(functools.reduce(jnp.add, kept), axis=0, keepdims=True)
        found.append((below(old + [p.astype(BF16) for p in kept[1:]] + new), total))
    return beside([f[0] for f in found]), beside([f[1] for f in found])


def softmax_tiles(q_ref, k_ext, v_ext, out_ref, first_tile, tiles, heads, present, meanwhile, stored):
    hd = q_ref.shape[1]
    rows = TILE * heads
    lanes = min(2 * TILE, rows)
    span = lanes // heads

    chunks = rows // lanes
    units = tiles * chunks
    values = {}

    def scores(u):
        t, i = divmod(u, chunks)
        if t >= tiles:
            return None
        keys = k_ext[pl.ds(pl.multiple_of((first_tile + t) * TILE + i * span, span), W + span), :]
        queries = q_ref[pl.ds(pl.multiple_of((first_tile + t) * rows + i * lanes, lanes), lanes), :]
        return nt(keys, queries)

    def output(u, found):
        t, i = divmod(u, chunks)
        weights, total = found
        if i == 0:
            values[t] = beside([v_ext[first_tile + t + j] for j in range(MIDS + 1)])
            if present is not None and t < MIDS:
                ones = jnp.ones((ONES, TILE), BF16)
                sides = [present if t + j < MIDS else ones for j in range(MIDS + 1)]
                values[t] = below([values[t], beside(sides)])
        out = nn(values[t], weights)
        if present is not None and t < MIDS:
            total = out[hd : hd + 1]
        out = (out[:hd] * (1.0 / total)).astype(BF16).T
        out_ref[pl.ds(pl.multiple_of((first_tile + t) * rows + i * lanes, lanes), lanes), :] = out
        if i == chunks - 1:
            stored(t)

    ahead, behind = DEPTH * chunks, LATE * chunks
    now = {u: scores(u) for u in range(ahead)}
    if meanwhile is not None:
        meanwhile()
    found = {}
    for u in range(units):
        now[u + ahead] = scores(u + ahead)
        found[u] = softmax_weights(now.pop(u), u % chunks, heads, hd)
        if u >= behind:
            output(u - behind, found.pop(u - behind))
    for u in range(units - behind, units):
        output(u, found.pop(u))


def gradient_tiles(q_ref, c_ref, v_ref, kft, state, grad, before, first_tile, tiles):
    heads = grad.shape[0]
    ahead = later_key(heads)
    group = 2 if tiles % 2 == 0 else 1
    now = state[...]
    starts, turned, backs, found, q = {}, {}, {}, {}, {}

    def load(t, now):
        if t >= tiles:
            return now
        here = at_tile(first_tile + t)
        turned[t] = below(head_rows(c_ref, first_tile + t, heads)).T
        q[t] = head_rows(q_ref, first_tile + t, heads)
        starts[t] = now.astype(BF16)
        return now + nn(kft[:, here], v_ref[here, :])

    def score(t):
        if t < tiles:
            back = nn(v_ref[at_tile(first_tile + t), :], turned[t])
            backs[t] = jnp.where(ahead, 0.0, back).astype(BF16)

    def gradient(t):
        left = beside([kft[:, at_tile(first_tile + t)], starts[t]])
        out = nn(left, below([backs[t], turned[t]])) * scale_of(before, first_tile + t, heads)
        found[t] = columns(out.astype(BF16))

    def add(ts):
        for h in range(heads):
            grad[h] += nn(beside([found[t][h] for t in ts]), below([q[t][h] for t in ts]))

    for t in range(LAG + 1):
        now = load(t, now)
    for t in range(LAG):
        score(t)
    for t in range(tiles):
        now = load(t + LAG + 1, now)
        score(t + LAG)
        gradient(t)
        if t and t % group == 0:
            add(range(t - group, t))
    add(range(tiles - group, tiles))
    state[...] = now


def linear_tiles(q_ref, kf_ref, vt_ref, maps_t, state, out_ref, first_token):
    heads, hd = q_ref.shape[1:]
    tiles = q_ref.shape[0] // TILE
    ahead = later_key(heads)
    group = 2 if tiles % 2 == 0 else 1
    q = pltpu.einshape("tha->hta", q_ref[...])
    now = state[...]
    starts, turned, inside, done = {}, {}, {}, []

    def load(t, now):
        if t >= tiles:
            return now
        if t % group == 0:
            rows = slice(t * TILE, (t + group) * TILE)
            features = [columns(nt(maps_t[h], q[h, rows]).astype(BF16)) for h in range(heads)]
            for i in range(group):
                turned[t + i] = beside([f[i] for f in features])
        starts[t] = now.astype(BF16)
        return now + nn(vt_ref[t], kf_ref[at_tile(t), :])

    def score(t):
        if t < tiles:
            scores = nn(kf_ref[at_tile(t), :], turned[t])
            inside[t] = jnp.where(ahead, 0.0, scores).astype(BF16)

    def output(t):
        left = beside([vt_ref[t], starts[t]])
        out = nn(left, below([inside[t], turned[t]])) * scale_of(first_token, t, heads)
        done.append([x.T for x in columns(out.astype(BF16))])

    for t in range(LAG + 1):
        now = load(t, now)
    for t in range(LAG):
        score(t)
    for t in range(tiles):
        now = load(t + LAG + 1, now)
        score(t + LAG)
        output(t)
    state[...] = now
    out_ref[...] = pltpu.einshape("hta->tha", below([below([d[h] for d in done])[None] for h in range(heads)]))


def first_kernel(
    count, step_tiles,
    q_hbm, c_hbm, k_hbm, v_hbm, key_map_ref,
    soft_hbm, vt_hbm, prefix_ref, mine_ref,
    q_all, c_all, k_ext, v_all, v_ext, kft, soft_all,
    local_sum, sums, halo, state, grad, pieces, pieces16, slots,
    load_sem, store_sem, sum_send, sum_recv, halo_send, halo_recv, piece_send, piece_recv,
):
    rank = lax.axis_index("seq")
    heads, hd = grad.shape[:2]
    tokens_here = v_all.shape[0]
    blocks = tokens_here // TILE
    share = hd // count
    half = blocks // 2
    before = rank * tokens_here

    def halo_copy(i):
        return pltpu.make_async_remote_copy(
            src_ref=(k_ext.at[pl.ds(tokens_here, W)], v_all.at[pl.ds(tokens_here - W, W)])[i],
            dst_ref=halo.at[i],
            send_sem=halo_send.at[i],
            recv_sem=halo_recv.at[i],
            device_id={"seq": rank + 1},
            device_id_type=MESH,
        )

    def sum_copy(k):
        return pltpu.make_async_remote_copy(
            src_ref=local_sum,
            dst_ref=sums.at[k - 1],
            send_sem=sum_send.at[k - 1],
            recv_sem=sum_recv.at[k - 1],
            device_id={"seq": rank + k},
            device_id_type=MESH,
        )

    def piece_copy(k):
        target = lax.rem(rank + k, count)
        return pltpu.make_async_remote_copy(
            src_ref=pieces16.at[target],
            dst_ref=slots.at[k - 1],
            send_sem=piece_send.at[k - 1],
            recv_sem=piece_recv.at[k - 1],
            device_id={"seq": target},
            device_id_type=MESH,
        )

    rows = TILE * heads
    lead = 3 * step_tiles // 4
    grain = 2

    def tiles_of(first, tiles):
        return pl.ds(first * rows, tiles * rows)

    first_part, late, soon = tiles_of(half, lead), tiles_of(half + lead, blocks - half - lead), tiles_of(0, half)
    loads = [
        pltpu.make_async_copy(source, target, load_sem.at[i])
        for i, (source, target) in enumerate([
            (k_hbm, k_ext.at[pl.ds(W, tokens_here)]),
            (v_hbm, v_all),
            (q_hbm.at[first_part], q_all.at[first_part]),
            (q_hbm.at[late], q_all.at[late]),
            (c_hbm, c_all),
            (q_hbm.at[soon], q_all.at[soon]),
        ])
    ]

    def soft_store(i):
        part = tiles_of(i * grain, grain)
        return pltpu.make_async_copy(soft_all.at[part], soft_hbm.at[part], store_sem.at[i])

    def softmax(first_tile, tiles, present=None, meanwhile=None):
        def stored(t):
            if (t + 1) % grain == 0:
                soft_store((first_tile + t) // grain).start()

        softmax_tiles(q_all, k_ext, v_ext, soft_all, first_tile, tiles, heads, present, meanwhile, stored)

    barrier = pltpu.get_barrier_semaphore()
    for k in range(1, count):
        pl.semaphore_signal(barrier, inc=1, device_id={"seq": lax.rem(rank + k, count)}, device_id_type=MESH)
    for load in loads[:3]:
        load.start()
    grad[...] = jnp.zeros_like(grad)
    state[...] = jnp.zeros_like(state)
    for load in loads[3:]:
        load.start()
    key_map_t = key_map_ref[...].astype(F32).T.astype(BF16)
    loads[0].wait()
    kft[...] = nt(key_map_t, k_ext[W:]).astype(BF16)
    loads[1].wait()
    loads[2].wait()
    for b in range(blocks):
        v_ext[MIDS + b] = v_all[b * TILE : (b + 1) * TILE, :].T

    def shard_sum():
        near, far = slice(0, tokens_here // 2), slice(tokens_here // 2, tokens_here)
        local_sum[...] = (nn(kft[:, near], v_all[near, :]) + nn(kft[:, far], v_all[far, :])).astype(BF16)

    softmax(half, lead, meanwhile=shard_sum)
    vt_store = pltpu.make_async_copy(v_ext.at[pl.ds(MIDS, blocks)], vt_hbm, store_sem.at[blocks // grain])
    vt_store.start()

    pl.semaphore_wait(barrier, count - 1)
    for k in range(1, count):
        @pl.when(rank + k < count)
        def _():
            sum_copy(k).start()
    @pl.when(rank + 1 < count)
    def _():
        halo_copy(0).start()
        halo_copy(1).start()

    loads[3].wait()
    softmax(half + lead, blocks - half - lead)

    for k in range(1, count):
        @pl.when(rank + k < count)
        def _():
            sum_copy(k).wait_send()
        @pl.when(rank >= k)
        def _():
            sum_copy(k).wait_recv()
            state[...] += sums[k - 1].astype(F32)
    prefix_ref[...] = state[...].T
    loads[4].wait()
    loads[5].wait()

    @pl.loop(0, blocks // (2 * step_tiles))
    def _(i):
        gradient_tiles(q_all, c_all, v_all, kft, state, grad, before, i * 2 * step_tiles, 2 * step_tiles)

    for h in range(heads):
        turned = grad[h].T
        for p in range(count):
            piece = turned[p * share : (p + 1) * share]
            pieces[p, :, h * hd : (h + 1) * hd] = piece
            pieces16[p, :, h * hd : (h + 1) * hd] = piece.astype(BF16)
    for k in range(1, count):
        piece_copy(k).start()

    @pl.when(rank + 1 < count)
    def _():
        halo_copy(0).wait_send()
        halo_copy(1).wait_send()
    @pl.when(rank >= 1)
    def _():
        halo_copy(0).wait_recv()
        halo_copy(1).wait_recv()
        k_ext[:W] = halo[0]
        for b in range(MIDS):
            v_ext[b] = halo[1, b * TILE : (b + 1) * TILE, :].T
    @pl.when(rank == 0)
    def _():
        k_ext[:W] = jnp.broadcast_to(k_ext[W : W + 1, :], (W, hd))
        v_ext[:MIDS] = jnp.zeros((MIDS,) + v_ext.shape[1:], BF16)
    softmax(0, half, jnp.where(rank == 0, jnp.zeros((ONES, TILE), F32), 1.0).astype(BF16))

    total = pieces[rank]
    for k in range(1, count):
        piece_copy(k).wait()
        total = total + slots[k - 1].astype(F32)
    mine_ref[...] = total
    for i in range(blocks // grain):
        soft_store(i).wait()
    vt_store.wait()


def last_kernel(
    steps,
    q_ref, k_first_ref, k_next_ref, vt_ref, soft_in_hbm, key_map_ref, maps_ref, prefix_ref, mine_in_ref,
    linear_ref, soft_hbm, mine_ref,
    kf, soft_all, maps_t, state, load_sem, store_sem,
):
    step = pl.program_id(0)
    heads, hd = q_ref.shape[1:]
    step_tokens = q_ref.shape[0]
    rows = step_tokens * heads

    def part(i):
        return pl.ds(pl.multiple_of(i * rows, rows), rows)

    def load(i):
        return pltpu.make_async_copy(soft_in_hbm.at[part(i)], soft_all.at[part(i)], load_sem.at[i])

    def store(i):
        return pltpu.make_async_copy(soft_all.at[part(i)], soft_hbm.at[part(i)], store_sem.at[i])

    @pl.when(step == 0)
    def _():
        for i in range(steps):
            load(i).start()
        kf[0] = nn(k_first_ref[...], key_map_ref[...]).astype(BF16)
        for h in range(heads):
            maps_t[h] = maps_ref[h].T
            mine_ref[:, h, :] = mine_in_ref[:, h * hd : (h + 1) * hd]
        state[...] = prefix_ref[...]

    @pl.when(step >= 1)
    def _():
        load(step - 1).wait()
        store(step - 1).start()

    @pl.when(step == steps - 1)
    def _():
        load(step).wait()
        store(step).start()

    first_token = (lax.axis_index("seq") * steps + step) * step_tokens
    linear_tiles(q_ref, kf.at[lax.rem(step, 2)], vt_ref, maps_t, state, linear_ref, first_token)
    kf[lax.rem(step + 1, 2)] = nn(k_next_ref[...], key_map_ref[...]).astype(BF16)

    @pl.when(step == steps - 1)
    def _():
        for i in range(steps):
            store(i).wait()


def per_device(queries, keys, values, query_maps, key_map, linear_cotangent):
    tokens_here, hd = keys.shape
    heads = queries.shape[1]
    count = lax.axis_size("seq")
    share = hd // count
    blocks = tokens_here // TILE
    step_tiles = 8
    steps = blocks // step_tiles
    flat = (tokens_here * heads, hd)
    dma = pltpu.SemaphoreType.DMA
    hbm = pl.BlockSpec(memory_space=pl.ANY)
    vmem = pl.BlockSpec(memory_space=pltpu.VMEM)

    rows16 = jax.ShapeDtypeStruct(flat, BF16)
    vt16 = jax.ShapeDtypeStruct((blocks, hd, TILE), BF16)
    square = jax.ShapeDtypeStruct((hd, hd), F32)
    piece = jax.ShapeDtypeStruct((share, heads * hd), F32)
    soft, values_t, prefix, mine = pl.pallas_call(
        functools.partial(first_kernel, count, step_tiles),
        in_specs=[hbm, hbm, hbm, hbm, vmem],
        out_specs=[hbm, hbm, vmem, vmem],
        out_shape=[rows16, vt16, square, piece],
        scratch_shapes=[
            pltpu.VMEM(flat, BF16),
            pltpu.VMEM(flat, BF16),
            pltpu.VMEM((tokens_here + W, hd), BF16),
            pltpu.VMEM((tokens_here, hd), BF16),
            pltpu.VMEM((blocks + MIDS, hd, TILE), BF16),
            pltpu.VMEM((hd, tokens_here), BF16),
            pltpu.VMEM(flat, BF16),
            pltpu.VMEM((hd, hd), BF16),
            pltpu.VMEM((count - 1, hd, hd), BF16),
            pltpu.VMEM((2, W, hd), BF16),
            pltpu.VMEM((hd, hd), F32),
            pltpu.VMEM((heads, hd, hd), F32),
            pltpu.VMEM((count, share, heads * hd), F32),
            pltpu.VMEM((count, share, heads * hd), BF16),
            pltpu.VMEM((count - 1, share, heads * hd), BF16),
            dma((6,)), dma((blocks // 2 + 1,)),
            dma((count - 1,)), dma((count - 1,)), dma((2,)), dma((2,)), dma((count - 1,)), dma((count - 1,)),
        ],
        compiler_params=pltpu.CompilerParams(collective_id=0, has_side_effects=True),
        name="softmax_and_gradient",
    )(queries.reshape(flat), linear_cotangent.reshape(flat), keys, values, key_map)

    once = lambda a: pl.BlockSpec(a.shape, lambda i: (0,) * len(a.shape), pipeline_mode=pl.Buffered(1))
    tokens = step_tiles * TILE
    along = pl.BlockSpec((tokens, heads, hd), lambda i: (i, 0, 0))
    final = jax.ShapeDtypeStruct((share, heads, hd), F32)
    linear, soft, mine = pl.pallas_call(
        functools.partial(last_kernel, steps),
        grid=(steps,),
        in_specs=[
            along,
            pl.BlockSpec((tokens, hd), lambda i: (0, 0), pipeline_mode=pl.Buffered(1)),
            pl.BlockSpec((tokens, hd), lambda i: (jnp.minimum(i + 1, steps - 1), 0)),
            pl.BlockSpec((step_tiles, hd, TILE), lambda i: (i, 0, 0)),
            hbm, once(key_map), once(query_maps), once(prefix), once(mine),
        ],
        out_specs=[along, hbm, once(final)],
        out_shape=[jax.ShapeDtypeStruct((tokens_here, heads, hd), BF16), rows16, final],
        scratch_shapes=[
            pltpu.VMEM((2, tokens, hd), BF16),
            pltpu.VMEM(flat, BF16),
            pltpu.VMEM((heads, hd, hd), BF16),
            pltpu.VMEM((hd, hd), F32),
            dma((steps,)), dma((steps,)),
        ],
        compiler_params=pltpu.CompilerParams(dimension_semantics=("arbitrary",)),
        name="linear",
    )(queries, keys, keys, values_t, soft, key_map, query_maps, prefix, mine)
    return soft.reshape(queries.shape), linear, mine


def solution(mesh):
    rows = P(("groups", "seq"), ("head", "rep"), None)
    return jax.shard_map(
        per_device,
        mesh=mesh,
        in_specs=(
            rows,
            P(("groups", "seq"), None),
            P(("groups", "seq"), None),
            P(("groups", "head", "rep"), None, None),
            P("groups", None),
            rows,
        ),
        out_specs=(rows, rows, rows),
        check_vma=False,
    )
```

```python
import functools

import jax
import jax.numpy as jnp
from jax import lax
from jax.experimental import pallas as pl
from jax.experimental.pallas import tpu as pltpu
from jax.sharding import PartitionSpec as P

W = 512
TILE = 128
MIDS = W // TILE
ONES = 16
LAG = 3
DEPTH = 2
LATE = 1
MESH = pl.DeviceIdType.MESH
F32 = jnp.float32
BF16 = jnp.bfloat16


def nt(a, b):
    return lax.dot_general(a, b, (((1,), (1,)), ((), ())), preferred_element_type=F32)


def nn(a, b):
    return jnp.dot(a, b, preferred_element_type=F32)


def beside(parts):
    return parts[0] if len(parts) == 1 else jnp.concatenate(parts, 1)


def below(parts):
    return parts[0] if len(parts) == 1 else jnp.concatenate(parts, 0)


def later_key(heads):
    shape = (TILE, TILE)
    one = lax.broadcasted_iota(jnp.int32, shape, 0) > lax.broadcasted_iota(jnp.int32, shape, 1)
    return beside([one] * heads)


def later_key_in_band(heads):
    shape = (TILE // heads, TILE)
    return lax.broadcasted_iota(jnp.int32, shape, 0) > lax.broadcasted_iota(jnp.int32, shape, 1) // heads


def columns(x):
    return [x[:, h : h + TILE] for h in range(0, x.shape[1], TILE)]


def at_tile(tile, rows=TILE):
    return pl.ds(pl.multiple_of(tile * rows, rows), rows)


def head_rows(ref, tile, heads):
    if heads == 1:
        return [ref[at_tile(tile), :]]
    own = ref.at[at_tile(tile, TILE * heads), :]
    return [own[pl.ds(h, TILE, stride=heads), :] for h in range(heads)]


def scale_of(before, tile, heads):
    token = lax.broadcasted_iota(jnp.int32, (1, TILE), 1) + (before + tile * TILE + 1)
    return beside([lax.rsqrt(token.astype(F32))] * heads)


def softmax_weights(chunk, part, heads, hd):
    scale = hd ** (-0.5) * 1.4426950408889634
    ahead = later_key_in_band(heads)
    span = TILE // heads
    skipped = part * (chunk.shape[0] - W)
    found = []
    for i, own in enumerate(columns(chunk)):
        a = skipped + i * span
        b = a + span
        rows = lambda start, stop: own[start - skipped : stop - skipped]
        edge = [rows(W, W + a)] * (a > 0) + [jnp.where(ahead, rows(a, b), rows(W + a, W + b))]
        edge = below(edge + [rows(b, TILE)] * (b < TILE))
        kept = [edge] + [rows(j * TILE, (j + 1) * TILE) for j in range(1, MIDS)]
        highest = jnp.max(functools.reduce(jnp.maximum, kept), axis=0, keepdims=True)
        kept = [jnp.exp2((p - highest) * scale) for p in kept]
        edge = kept[0]
        old = [jnp.zeros((a, TILE), BF16)] * (a > 0) + [jnp.where(ahead, edge[a:b], 0.0).astype(BF16)]
        new = [jnp.where(ahead, 0.0, edge[a:b]).astype(BF16)]
        if a > 0:
            new = [edge[:a].astype(BF16)] + new
        if b < TILE:
            old = old + [edge[b:].astype(BF16)]
            new = new + [jnp.zeros((TILE - b, TILE), BF16)]
        total = jnp.sum(functools.reduce(jnp.add, kept), axis=0, keepdims=True)
        found.append((below(old + [p.astype(BF16) for p in kept[1:]] + new), total))
    return beside([f[0] for f in found]), beside([f[1] for f in found])


def softmax_tiles(q_ref, k_ext, v_ext, out_ref, first_tile, tiles, heads, present, meanwhile, stored):
    hd = q_ref.shape[1]
    rows = TILE * heads
    lanes = min(2 * TILE, rows)
    span = lanes // heads

    chunks = rows // lanes
    units = tiles * chunks
    values = {}

    def scores(u):
        t, i = divmod(u, chunks)
        if t >= tiles:
            return None
        keys = k_ext[pl.ds(pl.multiple_of((first_tile + t) * TILE + i * span, span), W + span), :]
        queries = q_ref[pl.ds(pl.multiple_of((first_tile + t) * rows + i * lanes, lanes), lanes), :]
        return nt(keys, queries)

    def output(u, found):
        t, i = divmod(u, chunks)
        weights, total = found
        if i == 0:
            values[t] = beside([v_ext[first_tile + t + j] for j in range(MIDS + 1)])
            if present is not None and t < MIDS:
                ones = jnp.ones((ONES, TILE), BF16)
                sides = [present if t + j < MIDS else ones for j in range(MIDS + 1)]
                values[t] = below([values[t], beside(sides)])
        out = nn(values[t], weights)
        if present is not None and t < MIDS:
            total = out[hd : hd + 1]
        out = (out[:hd] * (1.0 / total)).astype(BF16).T
        out_ref[pl.ds(pl.multiple_of((first_tile + t) * rows + i * lanes, lanes), lanes), :] = out
        if i == chunks - 1:
            stored(t)

    ahead, behind = DEPTH * chunks, LATE * chunks
    now = {u: scores(u) for u in range(ahead)}
    if meanwhile is not None:
        meanwhile()
    found = {}
    for u in range(units):
        now[u + ahead] = scores(u + ahead)
        found[u] = softmax_weights(now.pop(u), u % chunks, heads, hd)
        if u >= behind:
            output(u - behind, found.pop(u - behind))
    for u in range(units - behind, units):
        output(u, found.pop(u))


def gradient_tiles(q_ref, c_ref, v_ref, kft, state, grad, before, first_tile, tiles):
    heads = grad.shape[0]
    ahead = later_key(heads)
    group = 2 if tiles % 2 == 0 else 1
    now = state[...]
    starts, turned, backs, found, q = {}, {}, {}, {}, {}

    def load(t, now):
        if t >= tiles:
            return now
        here = at_tile(first_tile + t)
        turned[t] = below(head_rows(c_ref, first_tile + t, heads)).T
        q[t] = head_rows(q_ref, first_tile + t, heads)
        starts[t] = now.astype(BF16)
        return now + nn(kft[:, here], v_ref[here, :])

    def score(t):
        if t < tiles:
            back = nn(v_ref[at_tile(first_tile + t), :], turned[t])
            backs[t] = jnp.where(ahead, 0.0, back).astype(BF16)

    def gradient(t):
        left = beside([kft[:, at_tile(first_tile + t)], starts[t]])
        out = nn(left, below([backs[t], turned[t]])) * scale_of(before, first_tile + t, heads)
        found[t] = columns(out.astype(BF16))

    def add(ts):
        for h in range(heads):
            grad[h] += nn(beside([found[t][h] for t in ts]), below([q[t][h] for t in ts]))

    for t in range(LAG + 1):
        now = load(t, now)
    for t in range(LAG):
        score(t)
    for t in range(tiles):
        now = load(t + LAG + 1, now)
        score(t + LAG)
        gradient(t)
        if t and t % group == 0:
            add(range(t - group, t))
    add(range(tiles - group, tiles))
    state[...] = now


def linear_tiles(q_ref, kf_ref, vt_ref, maps_t, state, out_ref, first_token):
    heads, hd = q_ref.shape[1:]
    tiles = q_ref.shape[0] // TILE
    ahead = later_key(heads)
    group = 2 if tiles % 2 == 0 else 1
    q = pltpu.einshape("tha->hta", q_ref[...])
    now = state[...]
    starts, turned, inside, done = {}, {}, {}, []

    def load(t, now):
        if t >= tiles:
            return now
        if t % group == 0:
            rows = slice(t * TILE, (t + group) * TILE)
            features = [columns(nt(maps_t[h], q[h, rows]).astype(BF16)) for h in range(heads)]
            for i in range(group):
                turned[t + i] = beside([f[i] for f in features])
        starts[t] = now.astype(BF16)
        return now + nn(vt_ref[t], kf_ref[at_tile(t), :])

    def score(t):
        if t < tiles:
            scores = nn(kf_ref[at_tile(t), :], turned[t])
            inside[t] = jnp.where(ahead, 0.0, scores).astype(BF16)

    def output(t):
        left = beside([vt_ref[t], starts[t]])
        out = nn(left, below([inside[t], turned[t]])) * scale_of(first_token, t, heads)
        done.append([x.T for x in columns(out.astype(BF16))])

    for t in range(LAG + 1):
        now = load(t, now)
    for t in range(LAG):
        score(t)
    for t in range(tiles):
        now = load(t + LAG + 1, now)
        score(t + LAG)
        output(t)
    state[...] = now
    out_ref[...] = pltpu.einshape("hta->tha", below([below([d[h] for d in done])[None] for h in range(heads)]))


def first_kernel(
    count, step_tiles,
    q_hbm, c_hbm, k_hbm, v_hbm, key_map_ref,
    soft_hbm, vt_hbm, prefix_ref, mine_ref,
    q_all, c_all, k_ext, v_all, v_ext, kft, soft_all,
    local_sum, sums, halo, state, grad, pieces, pieces16, slots,
    load_sem, store_sem, sum_send, sum_recv, halo_send, halo_recv, piece_send, piece_recv,
):
    rank = lax.axis_index("seq")
    heads, hd = grad.shape[:2]
    tokens_here = v_all.shape[0]
    blocks = tokens_here // TILE
    share = hd // count
    half = blocks // 2
    before = rank * tokens_here

    def halo_copy(i):
        return pltpu.make_async_remote_copy(
            src_ref=(k_ext.at[pl.ds(tokens_here, W)], v_all.at[pl.ds(tokens_here - W, W)])[i],
            dst_ref=halo.at[i],
            send_sem=halo_send.at[i],
            recv_sem=halo_recv.at[i],
            device_id={"seq": rank + 1},
            device_id_type=MESH,
        )

    def sum_copy(k):
        return pltpu.make_async_remote_copy(
            src_ref=local_sum,
            dst_ref=sums.at[k - 1],
            send_sem=sum_send.at[k - 1],
            recv_sem=sum_recv.at[k - 1],
            device_id={"seq": rank + k},
            device_id_type=MESH,
        )

    def piece_copy(k):
        target = lax.rem(rank + k, count)
        return pltpu.make_async_remote_copy(
            src_ref=pieces16.at[target],
            dst_ref=slots.at[k - 1],
            send_sem=piece_send.at[k - 1],
            recv_sem=piece_recv.at[k - 1],
            device_id={"seq": target},
            device_id_type=MESH,
        )

    rows = TILE * heads
    lead = 3 * step_tiles // 4
    grain = 2

    def tiles_of(first, tiles):
        return pl.ds(first * rows, tiles * rows)

    first_part, late, soon = tiles_of(half, lead), tiles_of(half + lead, blocks - half - lead), tiles_of(0, half)
    loads = [
        pltpu.make_async_copy(source, target, load_sem.at[i])
        for i, (source, target) in enumerate([
            (k_hbm, k_ext.at[pl.ds(W, tokens_here)]),
            (v_hbm, v_all),
            (q_hbm.at[first_part], q_all.at[first_part]),
            (q_hbm.at[late], q_all.at[late]),
            (c_hbm, c_all),
            (q_hbm.at[soon], q_all.at[soon]),
        ])
    ]

    def soft_store(i):
        part = tiles_of(i * grain, grain)
        return pltpu.make_async_copy(soft_all.at[part], soft_hbm.at[part], store_sem.at[i])

    def softmax(first_tile, tiles, present=None, meanwhile=None):
        def stored(t):
            if (t + 1) % grain == 0:
                soft_store((first_tile + t) // grain).start()

        softmax_tiles(q_all, k_ext, v_ext, soft_all, first_tile, tiles, heads, present, meanwhile, stored)

    barrier = pltpu.get_barrier_semaphore()
    for k in range(1, count):
        pl.semaphore_signal(barrier, inc=1, device_id={"seq": lax.rem(rank + k, count)}, device_id_type=MESH)
    for load in loads[:3]:
        load.start()
    grad[...] = jnp.zeros_like(grad)
    state[...] = jnp.zeros_like(state)
    for load in loads[3:]:
        load.start()
    key_map_t = key_map_ref[...].astype(F32).T.astype(BF16)
    loads[0].wait()
    kft[...] = nt(key_map_t, k_ext[W:]).astype(BF16)
    loads[1].wait()
    loads[2].wait()
    for b in range(blocks):
        v_ext[MIDS + b] = v_all[b * TILE : (b + 1) * TILE, :].T

    def shard_sum():
        near, far = slice(0, tokens_here // 2), slice(tokens_here // 2, tokens_here)
        local_sum[...] = (nn(kft[:, near], v_all[near, :]) + nn(kft[:, far], v_all[far, :])).astype(BF16)

    softmax(half, lead, meanwhile=shard_sum)
    vt_store = pltpu.make_async_copy(v_ext.at[pl.ds(MIDS, blocks)], vt_hbm, store_sem.at[blocks // grain])
    vt_store.start()

    pl.semaphore_wait(barrier, count - 1)
    for k in range(1, count):
        @pl.when(rank + k < count)
        def _():
            sum_copy(k).start()

    loads[3].wait()
    softmax(half + lead, blocks - half - lead)

    for k in range(1, count):
        @pl.when(rank + k < count)
        def _():
            sum_copy(k).wait_send()
        @pl.when(rank >= k)
        def _():
            sum_copy(k).wait_recv()
            state[...] += sums[k - 1].astype(F32)
    @pl.when(rank + 1 < count)
    def _():
        halo_copy(0).start()
        halo_copy(1).start()
    prefix_ref[...] = state[...].T
    loads[4].wait()
    loads[5].wait()

    @pl.loop(0, blocks // (2 * step_tiles))
    def _(i):
        gradient_tiles(q_all, c_all, v_all, kft, state, grad, before, i * 2 * step_tiles, 2 * step_tiles)

    for h in range(heads):
        turned = grad[h].T
        for p in range(count):
            piece = turned[p * share : (p + 1) * share]
            pieces[p, :, h * hd : (h + 1) * hd] = piece
            pieces16[p, :, h * hd : (h + 1) * hd] = piece.astype(BF16)
    for k in range(1, count):
        piece_copy(k).start()

    softmax(MIDS, half - MIDS)

    @pl.when(rank + 1 < count)
    def _():
        halo_copy(0).wait_send()
        halo_copy(1).wait_send()
    @pl.when(rank >= 1)
    def _():
        halo_copy(0).wait_recv()
        halo_copy(1).wait_recv()
        k_ext[:W] = halo[0]
        for b in range(MIDS):
            v_ext[b] = halo[1, b * TILE : (b + 1) * TILE, :].T
    @pl.when(rank == 0)
    def _():
        k_ext[:W] = jnp.broadcast_to(k_ext[W : W + 1, :], (W, hd))
        v_ext[:MIDS] = jnp.zeros((MIDS,) + v_ext.shape[1:], BF16)
    softmax(0, MIDS, jnp.where(rank == 0, jnp.zeros((ONES, TILE), F32), 1.0).astype(BF16))

    total = pieces[rank]
    for k in range(1, count):
        piece_copy(k).wait()
        total = total + slots[k - 1].astype(F32)
    mine_ref[...] = total
    for i in range(blocks // grain):
        soft_store(i).wait()
    vt_store.wait()


def last_kernel(
    steps,
    q_ref, k_first_ref, k_next_ref, vt_ref, soft_in_hbm, key_map_ref, maps_ref, prefix_ref, mine_in_ref,
    linear_ref, soft_hbm, mine_ref,
    kf, soft_all, maps_t, state, load_sem, store_sem,
):
    step = pl.program_id(0)
    heads, hd = q_ref.shape[1:]
    step_tokens = q_ref.shape[0]
    rows = step_tokens * heads

    def part(i):
        return pl.ds(pl.multiple_of(i * rows, rows), rows)

    def load(i):
        return pltpu.make_async_copy(soft_in_hbm.at[part(i)], soft_all.at[part(i)], load_sem.at[i])

    def store(i):
        return pltpu.make_async_copy(soft_all.at[part(i)], soft_hbm.at[part(i)], store_sem.at[i])

    @pl.when(step == 0)
    def _():
        for i in range(steps):
            load(i).start()
        kf[0] = nn(k_first_ref[...], key_map_ref[...]).astype(BF16)
        for h in range(heads):
            maps_t[h] = maps_ref[h].T
            mine_ref[:, h, :] = mine_in_ref[:, h * hd : (h + 1) * hd]
        state[...] = prefix_ref[...]

    @pl.when(step >= 1)
    def _():
        load(step - 1).wait()
        store(step - 1).start()

    @pl.when(step == steps - 1)
    def _():
        load(step).wait()
        store(step).start()

    first_token = (lax.axis_index("seq") * steps + step) * step_tokens
    linear_tiles(q_ref, kf.at[lax.rem(step, 2)], vt_ref, maps_t, state, linear_ref, first_token)
    kf[lax.rem(step + 1, 2)] = nn(k_next_ref[...], key_map_ref[...]).astype(BF16)

    @pl.when(step == steps - 1)
    def _():
        for i in range(steps):
            store(i).wait()


def per_device(queries, keys, values, query_maps, key_map, linear_cotangent):
    tokens_here, hd = keys.shape
    heads = queries.shape[1]
    count = lax.axis_size("seq")
    share = hd // count
    blocks = tokens_here // TILE
    step_tiles = 8
    steps = blocks // step_tiles
    flat = (tokens_here * heads, hd)
    dma = pltpu.SemaphoreType.DMA
    hbm = pl.BlockSpec(memory_space=pl.ANY)
    vmem = pl.BlockSpec(memory_space=pltpu.VMEM)

    rows16 = jax.ShapeDtypeStruct(flat, BF16)
    vt16 = jax.ShapeDtypeStruct((blocks, hd, TILE), BF16)
    square = jax.ShapeDtypeStruct((hd, hd), F32)
    piece = jax.ShapeDtypeStruct((share, heads * hd), F32)
    soft, values_t, prefix, mine = pl.pallas_call(
        functools.partial(first_kernel, count, step_tiles),
        in_specs=[hbm, hbm, hbm, hbm, vmem],
        out_specs=[hbm, hbm, vmem, vmem],
        out_shape=[rows16, vt16, square, piece],
        scratch_shapes=[
            pltpu.VMEM(flat, BF16),
            pltpu.VMEM(flat, BF16),
            pltpu.VMEM((tokens_here + W, hd), BF16),
            pltpu.VMEM((tokens_here, hd), BF16),
            pltpu.VMEM((blocks + MIDS, hd, TILE), BF16),
            pltpu.VMEM((hd, tokens_here), BF16),
            pltpu.VMEM(flat, BF16),
            pltpu.VMEM((hd, hd), BF16),
            pltpu.VMEM((count - 1, hd, hd), BF16),
            pltpu.VMEM((2, W, hd), BF16),
            pltpu.VMEM((hd, hd), F32),
            pltpu.VMEM((heads, hd, hd), F32),
            pltpu.VMEM((count, share, heads * hd), F32),
            pltpu.VMEM((count, share, heads * hd), BF16),
            pltpu.VMEM((count - 1, share, heads * hd), BF16),
            dma((6,)), dma((blocks // 2 + 1,)),
            dma((count - 1,)), dma((count - 1,)), dma((2,)), dma((2,)), dma((count - 1,)), dma((count - 1,)),
        ],
        compiler_params=pltpu.CompilerParams(collective_id=0, has_side_effects=True),
        name="softmax_and_gradient",
    )(queries.reshape(flat), linear_cotangent.reshape(flat), keys, values, key_map)

    once = lambda a: pl.BlockSpec(a.shape, lambda i: (0,) * len(a.shape), pipeline_mode=pl.Buffered(1))
    tokens = step_tiles * TILE
    along = pl.BlockSpec((tokens, heads, hd), lambda i: (i, 0, 0))
    final = jax.ShapeDtypeStruct((share, heads, hd), F32)
    linear, soft, mine = pl.pallas_call(
        functools.partial(last_kernel, steps),
        grid=(steps,),
        in_specs=[
            along,
            pl.BlockSpec((tokens, hd), lambda i: (0, 0), pipeline_mode=pl.Buffered(1)),
            pl.BlockSpec((tokens, hd), lambda i: (jnp.minimum(i + 1, steps - 1), 0)),
            pl.BlockSpec((step_tiles, hd, TILE), lambda i: (i, 0, 0)),
            hbm, once(key_map), once(query_maps), once(prefix), once(mine),
        ],
        out_specs=[along, hbm, once(final)],
        out_shape=[jax.ShapeDtypeStruct((tokens_here, heads, hd), BF16), rows16, final],
        scratch_shapes=[
            pltpu.VMEM((2, tokens, hd), BF16),
            pltpu.VMEM(flat, BF16),
            pltpu.VMEM((heads, hd, hd), BF16),
            pltpu.VMEM((hd, hd), F32),
            dma((steps,)), dma((steps,)),
        ],
        compiler_params=pltpu.CompilerParams(dimension_semantics=("arbitrary",)),
        name="linear",
    )(queries, keys, keys, values_t, soft, key_map, query_maps, prefix, mine)
    return soft.reshape(queries.shape), linear, mine


def solution(mesh):
    rows = P(("groups", "seq"), ("head", "rep"), None)
    return jax.shard_map(
        per_device,
        mesh=mesh,
        in_specs=(
            rows,
            P(("groups", "seq"), None),
            P(("groups", "seq"), None),
            P(("groups", "head", "rep"), None, None),
            P("groups", None),
            rows,
        ),
        out_specs=(rows, rows, rows),
        check_vma=False,
    )
```

```python
import functools

import jax
import jax.numpy as jnp
from jax import lax
from jax.experimental import pallas as pl
from jax.experimental.pallas import tpu as pltpu
from jax.sharding import PartitionSpec as P

W = 512
TILE = 128
MIDS = W // TILE
ONES = 16
LAG = 3
DEPTH = 2
LATE = 1
MESH = pl.DeviceIdType.MESH
F32 = jnp.float32
BF16 = jnp.bfloat16


def nt(a, b):
    return lax.dot_general(a, b, (((1,), (1,)), ((), ())), preferred_element_type=F32)


def nn(a, b):
    return jnp.dot(a, b, preferred_element_type=F32)


def beside(parts):
    return parts[0] if len(parts) == 1 else jnp.concatenate(parts, 1)


def below(parts):
    return parts[0] if len(parts) == 1 else jnp.concatenate(parts, 0)


def later_key(heads):
    shape = (TILE, TILE)
    one = lax.broadcasted_iota(jnp.int32, shape, 0) > lax.broadcasted_iota(jnp.int32, shape, 1)
    return beside([one] * heads)


def later_key_in_band(heads):
    shape = (TILE // heads, TILE)
    return lax.broadcasted_iota(jnp.int32, shape, 0) > lax.broadcasted_iota(jnp.int32, shape, 1) // heads


def columns(x):
    return [x[:, h : h + TILE] for h in range(0, x.shape[1], TILE)]


def at_tile(tile, rows=TILE):
    return pl.ds(pl.multiple_of(tile * rows, rows), rows)


def head_rows(ref, tile, heads):
    if heads == 1:
        return [ref[at_tile(tile), :]]
    own = ref.at[at_tile(tile, TILE * heads), :]
    return [own[pl.ds(h, TILE, stride=heads), :] for h in range(heads)]


def scale_of(before, tile, heads):
    token = lax.broadcasted_iota(jnp.int32, (1, TILE), 1) + (before + tile * TILE + 1)
    return beside([lax.rsqrt(token.astype(F32))] * heads)


def softmax_weights(chunk, part, heads, hd):
    scale = hd ** (-0.5) * 1.4426950408889634
    ahead = later_key_in_band(heads)
    span = TILE // heads
    skipped = part * (chunk.shape[0] - W)
    found = []
    for i, own in enumerate(columns(chunk)):
        a = skipped + i * span
        b = a + span
        rows = lambda start, stop: own[start - skipped : stop - skipped]
        edge = [rows(W, W + a)] * (a > 0) + [jnp.where(ahead, rows(a, b), rows(W + a, W + b))]
        edge = below(edge + [rows(b, TILE)] * (b < TILE))
        kept = [edge] + [rows(j * TILE, (j + 1) * TILE) for j in range(1, MIDS)]
        highest = jnp.max(functools.reduce(jnp.maximum, kept), axis=0, keepdims=True)
        kept = [jnp.exp2((p - highest) * scale) for p in kept]
        edge = kept[0]
        old = [jnp.zeros((a, TILE), BF16)] * (a > 0) + [jnp.where(ahead, edge[a:b], 0.0).astype(BF16)]
        new = [jnp.where(ahead, 0.0, edge[a:b]).astype(BF16)]
        if a > 0:
            new = [edge[:a].astype(BF16)] + new
        if b < TILE:
            old = old + [edge[b:].astype(BF16)]
            new = new + [jnp.zeros((TILE - b, TILE), BF16)]
        total = jnp.sum(functools.reduce(jnp.add, kept), axis=0, keepdims=True)
        found.append((below(old + [p.astype(BF16) for p in kept[1:]] + new), total))
    return beside([f[0] for f in found]), beside([f[1] for f in found])


def softmax_parts(q_ref, k_ext, v_ext, out_ref, q_tile, first_tile, heads, sides):
    hd = q_ref.shape[1]
    rows = TILE * heads
    lanes = min(2 * TILE, rows)
    span = lanes // heads
    chunks = rows // lanes
    values = {}

    def place(tile, i):
        return pl.ds(pl.multiple_of(tile * rows + i * lanes, lanes), lanes)

    def scores(u):
        t, i = divmod(u, chunks)
        keys = k_ext[pl.ds(pl.multiple_of((first_tile + t) * TILE + i * span, span), W + span), :]
        return nt(keys, q_ref[place(q_tile + t, i), :])

    def weights(u, found):
        return softmax_weights(found, u % chunks, heads, hd)

    def output(u, found):
        t, i = divmod(u, chunks)
        weights, total = found
        if i == 0:
            values[t] = beside([v_ext[first_tile + t + j] for j in range(MIDS + 1)])
            if sides is not None:
                values[t] = below([values[t], beside(sides)])
        out = nn(values[t], weights)
        if sides is not None:
            total = out[hd : hd + 1]
        out_ref[place(first_tile + t, i), :] = (out[:hd] * (1.0 / total)).astype(BF16).T

    return chunks, scores, weights, output


def softmax_tiles(q_ref, k_ext, v_ext, out_ref, first_tile, tiles, heads, meanwhile, stored):
    chunks, scores, weights, output = softmax_parts(
        q_ref, k_ext, v_ext, out_ref, first_tile, first_tile, heads, None
    )
    units = tiles * chunks
    ahead, behind = DEPTH * chunks, LATE * chunks

    def finish(u):
        output(u, found.pop(u))
        if (u + 1) % chunks == 0:
            stored(u // chunks)

    now = {u: scores(u) for u in range(ahead)}
    if meanwhile is not None:
        meanwhile()
    found = {}
    for u in range(units):
        if u + ahead < units:
            now[u + ahead] = scores(u + ahead)
        found[u] = weights(u, now.pop(u))
        if u >= behind:
            finish(u - behind)
    for u in range(units - behind, units):
        finish(u)


def gradient_tiles(q_ref, c_ref, v_ref, kft, state, grad, before, first_tile, tiles):
    heads = grad.shape[0]
    ahead = later_key(heads)
    group = 2 if tiles % 2 == 0 else 1
    now = state[...]
    starts, turned, backs, found, q = {}, {}, {}, {}, {}

    def load(t, now):
        if t >= tiles:
            return now
        here = at_tile(first_tile + t)
        turned[t] = below(head_rows(c_ref, first_tile + t, heads)).T
        q[t] = head_rows(q_ref, first_tile + t, heads)
        starts[t] = now.astype(BF16)
        return now + nn(kft[:, here], v_ref[here, :])

    def score(t):
        if t < tiles:
            back = nn(v_ref[at_tile(first_tile + t), :], turned[t])
            backs[t] = jnp.where(ahead, 0.0, back).astype(BF16)

    def gradient(t):
        left = beside([kft[:, at_tile(first_tile + t)], starts[t]])
        out = nn(left, below([backs[t], turned[t]])) * scale_of(before, first_tile + t, heads)
        found[t] = columns(out.astype(BF16))

    def add(ts):
        for h in range(heads):
            grad[h] += nn(beside([found[t][h] for t in ts]), below([q[t][h] for t in ts]))

    for t in range(LAG + 1):
        now = load(t, now)
    for t in range(LAG):
        score(t)
    for t in range(tiles):
        now = load(t + LAG + 1, now)
        score(t + LAG)
        gradient(t)
        if t and t % group == 0:
            add(range(t - group, t))
    add(range(tiles - group, tiles))
    state[...] = now


def linear_tiles(q_ref, kf_ref, vt_ref, maps_t, state, out_ref, first_token, between):
    heads, hd = q_ref.shape[1:]
    tiles = q_ref.shape[0] // TILE
    ahead = later_key(heads)
    group = 2 if tiles % 2 == 0 else 1
    q = pltpu.einshape("tha->hta", q_ref[...])
    now = state[...]
    starts, turned, inside, done = {}, {}, {}, []

    def load(t, now):
        if t >= tiles:
            return now
        if t % group == 0:
            rows = slice(t * TILE, (t + group) * TILE)
            features = [columns(nt(maps_t[h], q[h, rows]).astype(BF16)) for h in range(heads)]
            for i in range(group):
                turned[t + i] = beside([f[i] for f in features])
        starts[t] = now.astype(BF16)
        return now + nn(vt_ref[t], kf_ref[at_tile(t), :])

    def score(t):
        if t < tiles:
            scores = nn(kf_ref[at_tile(t), :], turned[t])
            inside[t] = jnp.where(ahead, 0.0, scores).astype(BF16)

    def output(t):
        left = beside([vt_ref[t], starts[t]])
        out = nn(left, below([inside[t], turned[t]])) * scale_of(first_token, t, heads)
        done.append([x.T for x in columns(out.astype(BF16))])

    for t in range(LAG + 1):
        now = load(t, now)
    for t in range(LAG):
        score(t)
    for t in range(tiles):
        now = load(t + LAG + 1, now)
        score(t + LAG)
        output(t)
        between(t)
    state[...] = now
    out_ref[...] = pltpu.einshape("hta->tha", below([below([d[h] for d in done])[None] for h in range(heads)]))


def first_kernel(
    count, step_tiles,
    q_hbm, c_hbm, k_hbm, v_hbm, key_map_ref,
    soft_hbm, vt_hbm, prefix_ref, mine_ref, rim_ref,
    q_all, c_all, k_ext, v_all, v_ext, kft, soft_all,
    local_sum, sums, halo, state, grad, pieces, pieces16, slots,
    load_sem, store_sem, sum_send, sum_recv, halo_send, halo_recv, piece_send, piece_recv,
):
    rank = lax.axis_index("seq")
    heads, hd = grad.shape[:2]
    tokens_here = v_all.shape[0]
    blocks = tokens_here // TILE
    share = hd // count
    half = blocks // 2
    before = rank * tokens_here

    def halo_copy(i):
        return pltpu.make_async_remote_copy(
            src_ref=(k_ext.at[pl.ds(tokens_here, W)], v_all.at[pl.ds(tokens_here - W, W)])[i],
            dst_ref=halo.at[i],
            send_sem=halo_send.at[i],
            recv_sem=halo_recv.at[i],
            device_id={"seq": rank + 1},
            device_id_type=MESH,
        )

    def sum_copy(k):
        return pltpu.make_async_remote_copy(
            src_ref=local_sum,
            dst_ref=sums.at[k - 1],
            send_sem=sum_send.at[k - 1],
            recv_sem=sum_recv.at[k - 1],
            device_id={"seq": rank + k},
            device_id_type=MESH,
        )

    def piece_copy(k):
        target = lax.rem(rank + k, count)
        return pltpu.make_async_remote_copy(
            src_ref=pieces16.at[target],
            dst_ref=slots.at[k - 1],
            send_sem=piece_send.at[k - 1],
            recv_sem=piece_recv.at[k - 1],
            device_id={"seq": target},
            device_id_type=MESH,
        )

    rows = TILE * heads
    lead = 3 * step_tiles // 4
    grain = 2

    def tiles_of(first, tiles):
        return pl.ds(first * rows, tiles * rows)

    first_part, late, soon = tiles_of(half, lead), tiles_of(half + lead, blocks - half - lead), tiles_of(0, half)
    loads = [
        pltpu.make_async_copy(source, target, load_sem.at[i])
        for i, (source, target) in enumerate([
            (k_hbm, k_ext.at[pl.ds(W, tokens_here)]),
            (v_hbm, v_all),
            (q_hbm.at[first_part], q_all.at[first_part]),
            (q_hbm.at[late], q_all.at[late]),
            (c_hbm, c_all),
            (q_hbm.at[soon], q_all.at[soon]),
        ])
    ]

    def soft_store(i):
        part = tiles_of(i * grain, grain)
        return pltpu.make_async_copy(soft_all.at[part], soft_hbm.at[part], store_sem.at[i])

    def softmax(first_tile, tiles, meanwhile=None):
        def stored(t):
            if (t + 1) % grain == 0:
                soft_store((first_tile + t) // grain).start()

        softmax_tiles(q_all, k_ext, v_ext, soft_all, first_tile, tiles, heads, meanwhile, stored)

    barrier = pltpu.get_barrier_semaphore()
    for k in range(1, count):
        pl.semaphore_signal(barrier, inc=1, device_id={"seq": lax.rem(rank + k, count)}, device_id_type=MESH)
    for load in loads[:3]:
        load.start()
    grad[...] = jnp.zeros_like(grad)
    state[...] = jnp.zeros_like(state)
    for load in loads[3:]:
        load.start()
    key_map_t = key_map_ref[...].astype(F32).T.astype(BF16)
    loads[0].wait()
    kft[...] = nt(key_map_t, k_ext[W:]).astype(BF16)
    loads[1].wait()
    loads[2].wait()
    for b in range(blocks):
        v_ext[MIDS + b] = v_all[b * TILE : (b + 1) * TILE, :].T

    def shard_sum():
        near, far = slice(0, tokens_here // 2), slice(tokens_here // 2, tokens_here)
        local_sum[...] = (nn(kft[:, near], v_all[near, :]) + nn(kft[:, far], v_all[far, :])).astype(BF16)

    softmax(half, lead, meanwhile=shard_sum)
    vt_store = pltpu.make_async_copy(v_ext.at[pl.ds(MIDS, blocks)], vt_hbm, store_sem.at[blocks // grain])
    vt_store.start()

    pl.semaphore_wait(barrier, count - 1)
    for k in reversed(range(1, count)):
        @pl.when(rank + k < count)
        def _():
            sum_copy(k).start()

    loads[3].wait()
    softmax(half + lead, blocks - half - lead)

    for k in range(1, count):
        @pl.when(rank + k < count)
        def _():
            sum_copy(k).wait_send()
        @pl.when(rank >= k)
        def _():
            sum_copy(k).wait_recv()
            state[...] += sums[k - 1].astype(F32)
    @pl.when(rank + 1 < count)
    def _():
        halo_copy(0).start()
        halo_copy(1).start()
    prefix_ref[...] = state[...].T
    loads[4].wait()
    loads[5].wait()

    @pl.loop(0, blocks // (2 * step_tiles))
    def _(i):
        gradient_tiles(q_all, c_all, v_all, kft, state, grad, before, i * 2 * step_tiles, 2 * step_tiles)

    for h in range(heads):
        turned = grad[h].T
        for p in range(count):
            piece = turned[p * share : (p + 1) * share]
            pieces[p, :, h * hd : (h + 1) * hd] = piece
            pieces16[p, :, h * hd : (h + 1) * hd] = piece.astype(BF16)
    for k in reversed(range(1, count)):
        piece_copy(k).start()

    softmax(MIDS, half - MIDS)

    @pl.when(rank + 1 < count)
    def _():
        halo_copy(0).wait_send()
        halo_copy(1).wait_send()
    @pl.when(rank >= 1)
    def _():
        halo_copy(0).wait_recv()
        halo_copy(1).wait_recv()
        rim_ref[...] = halo[...]
    @pl.when(rank == 0)
    def _():
        rim_ref[0] = jnp.broadcast_to(k_ext[W : W + 1, :], (W, hd))
        rim_ref[1] = jnp.zeros((W, hd), BF16)

    total = pieces[rank]
    for k in range(1, count):
        piece_copy(k).wait()
        total = total + slots[k - 1].astype(F32)
    mine_ref[...] = total
    for i in range(MIDS // grain, blocks // grain):
        soft_store(i).wait()
    vt_store.wait()


def last_kernel(
    steps,
    q_ref, q_own_ref, k_first_ref, k_next_ref, vt_ref, vt_first_ref, soft_in_hbm,
    key_map_ref, maps_ref, prefix_ref, mine_in_ref, rim_ref,
    linear_ref, soft_hbm, mine_ref,
    kf, soft_all, k_ext, v_ext, maps_t, state, load_sem, store_sem, own_sem,
):
    step = pl.program_id(0)
    rank = lax.axis_index("seq")
    heads, hd = q_ref.shape[1:]
    step_tokens = q_ref.shape[0]
    rows = TILE * heads
    passed = (soft_all.shape[0] // rows - MIDS) // steps * rows

    def part(i):
        return pl.ds(pl.multiple_of(MIDS * rows + i * passed, rows), passed)

    def load(i):
        return pltpu.make_async_copy(soft_in_hbm.at[part(i)], soft_all.at[part(i)], load_sem.at[i])

    def store(i):
        return pltpu.make_async_copy(soft_all.at[part(i)], soft_hbm.at[part(i)], store_sem.at[i])

    def store_own(i):
        own = at_tile(i, rows)
        return pltpu.make_async_copy(soft_all.at[own], soft_hbm.at[own], own_sem.at[i])

    @pl.when(step == 0)
    def _():
        load(0).start()
        kf[0] = nn(k_first_ref[...], key_map_ref[...]).astype(BF16)
        k_ext[:W] = rim_ref[0]
        k_ext[W:] = k_first_ref[:W]
        for b in range(MIDS):
            v_ext[b] = rim_ref[1, b * TILE : (b + 1) * TILE, :].T
            v_ext[MIDS + b] = vt_first_ref[b]
        for h in range(heads):
            maps_t[h] = maps_ref[h].T
            mine_ref[:, h, :] = mine_in_ref[:, h * hd : (h + 1) * hd]
        state[...] = prefix_ref[...]

    @pl.when(step + 1 < steps)
    def _():
        load(step + 1).start()

    @pl.when(step >= 1)
    def _():
        load(step - 1).wait()
        store(step - 1).start()

    @pl.when(step == steps - 1)
    def _():
        load(step).wait()
        store(step).start()

    sides = [
        jnp.where((rank == 0) & (step + j < MIDS), jnp.zeros((ONES, TILE), F32), 1.0).astype(BF16)
        for j in range(MIDS + 1)
    ]
    chunks, scores, weights, output = softmax_parts(
        q_own_ref, k_ext, v_ext, soft_all, 0, step, heads, sides
    )
    found = [weights(u, s) for u, s in enumerate([scores(u) for u in range(chunks)])]

    def between(t):
        if t % 2 == 0 and t // 2 < chunks:
            output(t // 2, found[t // 2])

    first_token = (rank * steps + step) * step_tokens
    linear_tiles(
        q_ref, kf.at[lax.rem(step, 2)], vt_ref, maps_t, state, linear_ref, first_token, between
    )
    kf[lax.rem(step + 1, 2)] = nn(k_next_ref[...], key_map_ref[...]).astype(BF16)
    store_own(step).start()

    @pl.when(step == steps - 1)
    def _():
        for i in range(steps):
            store(i).wait()
            store_own(i).wait()


def per_device(queries, keys, values, query_maps, key_map, linear_cotangent):
    tokens_here, hd = keys.shape
    heads = queries.shape[1]
    count = lax.axis_size("seq")
    share = hd // count
    blocks = tokens_here // TILE
    step_tiles = 8
    steps = blocks // step_tiles
    flat = (tokens_here * heads, hd)
    dma = pltpu.SemaphoreType.DMA
    hbm = pl.BlockSpec(memory_space=pl.ANY)
    vmem = pl.BlockSpec(memory_space=pltpu.VMEM)

    rows16 = jax.ShapeDtypeStruct(flat, BF16)
    vt16 = jax.ShapeDtypeStruct((blocks, hd, TILE), BF16)
    square = jax.ShapeDtypeStruct((hd, hd), F32)
    piece = jax.ShapeDtypeStruct((share, heads * hd), F32)
    soft, values_t, prefix, mine, rim = pl.pallas_call(
        functools.partial(first_kernel, count, step_tiles),
        in_specs=[hbm, hbm, hbm, hbm, vmem],
        out_specs=[hbm, hbm, vmem, vmem, vmem],
        out_shape=[rows16, vt16, square, piece, jax.ShapeDtypeStruct((2, W, hd), BF16)],
        scratch_shapes=[
            pltpu.VMEM(flat, BF16),
            pltpu.VMEM(flat, BF16),
            pltpu.VMEM((tokens_here + W, hd), BF16),
            pltpu.VMEM((tokens_here, hd), BF16),
            pltpu.VMEM((blocks + MIDS, hd, TILE), BF16),
            pltpu.VMEM((hd, tokens_here), BF16),
            pltpu.VMEM(flat, BF16),
            pltpu.VMEM((hd, hd), BF16),
            pltpu.VMEM((count - 1, hd, hd), BF16),
            pltpu.VMEM((2, W, hd), BF16),
            pltpu.VMEM((hd, hd), F32),
            pltpu.VMEM((heads, hd, hd), F32),
            pltpu.VMEM((count, share, heads * hd), F32),
            pltpu.VMEM((count, share, heads * hd), BF16),
            pltpu.VMEM((count - 1, share, heads * hd), BF16),
            dma((6,)), dma((blocks // 2 + 1,)),
            dma((count - 1,)), dma((count - 1,)), dma((2,)), dma((2,)), dma((count - 1,)), dma((count - 1,)),
        ],
        compiler_params=pltpu.CompilerParams(collective_id=0, has_side_effects=True),
        name="softmax_and_gradient",
    )(queries.reshape(flat), linear_cotangent.reshape(flat), keys, values, key_map)

    once = lambda a: pl.BlockSpec(a.shape, lambda i: (0,) * len(a.shape), pipeline_mode=pl.Buffered(1))
    tokens = step_tiles * TILE
    along = pl.BlockSpec((tokens, heads, hd), lambda i: (i, 0, 0))
    final = jax.ShapeDtypeStruct((share, heads, hd), F32)
    linear, soft, mine = pl.pallas_call(
        functools.partial(last_kernel, steps),
        grid=(steps,),
        in_specs=[
            along,
            pl.BlockSpec((TILE * heads, hd), lambda i: (i, 0)),
            pl.BlockSpec((tokens, hd), lambda i: (0, 0), pipeline_mode=pl.Buffered(1)),
            pl.BlockSpec((tokens, hd), lambda i: (jnp.minimum(i + 1, steps - 1), 0)),
            pl.BlockSpec((step_tiles, hd, TILE), lambda i: (i, 0, 0)),
            pl.BlockSpec((MIDS, hd, TILE), lambda i: (0, 0, 0), pipeline_mode=pl.Buffered(1)),
            hbm, once(key_map), once(query_maps), once(prefix), once(mine), once(rim),
        ],
        out_specs=[along, hbm, once(final)],
        out_shape=[jax.ShapeDtypeStruct((tokens_here, heads, hd), BF16), rows16, final],
        scratch_shapes=[
            pltpu.VMEM((2, tokens, hd), BF16),
            pltpu.VMEM(flat, BF16),
            pltpu.VMEM((2 * W, hd), BF16),
            pltpu.VMEM((2 * MIDS, hd, TILE), BF16),
            pltpu.VMEM((heads, hd, hd), BF16),
            pltpu.VMEM((hd, hd), F32),
            dma((steps,)), dma((steps,)), dma((steps,)),
        ],
        compiler_params=pltpu.CompilerParams(dimension_semantics=("arbitrary",)),
        name="linear",
    )(
        queries, queries.reshape(flat), keys, keys, values_t, values_t, soft,
        key_map, query_maps, prefix, mine, rim,
    )
    return soft.reshape(queries.shape), linear, mine


def solution(mesh):
    rows = P(("groups", "seq"), ("head", "rep"), None)
    return jax.shard_map(
        per_device,
        mesh=mesh,
        in_specs=(
            rows,
            P(("groups", "seq"), None),
            P(("groups", "seq"), None),
            P(("groups", "head", "rep"), None, None),
            P("groups", None),
            rows,
        ),
        out_specs=(rows, rows, rows),
        check_vma=False,
    )
```

```python
import functools

import jax
import jax.numpy as jnp
from jax import lax
from jax.experimental import pallas as pl
from jax.experimental.pallas import tpu as pltpu
from jax.sharding import PartitionSpec as P

W = 512
TILE = 128
MIDS = W // TILE
ONES = 16
LAG = 3
DEPTH = 2
LATE = 1
MESH = pl.DeviceIdType.MESH
F32 = jnp.float32
BF16 = jnp.bfloat16


def nt(a, b):
    return lax.dot_general(a, b, (((1,), (1,)), ((), ())), preferred_element_type=F32)


def nn(a, b):
    return jnp.dot(a, b, preferred_element_type=F32)


def beside(parts):
    return parts[0] if len(parts) == 1 else jnp.concatenate(parts, 1)


def below(parts):
    return parts[0] if len(parts) == 1 else jnp.concatenate(parts, 0)


def later_key(heads):
    shape = (TILE, TILE)
    one = lax.broadcasted_iota(jnp.int32, shape, 0) > lax.broadcasted_iota(jnp.int32, shape, 1)
    return beside([one] * heads)


def later_key_in_band(heads):
    shape = (TILE // heads, TILE)
    return lax.broadcasted_iota(jnp.int32, shape, 0) > lax.broadcasted_iota(jnp.int32, shape, 1) // heads


def columns(x):
    return [x[:, h : h + TILE] for h in range(0, x.shape[1], TILE)]


def at_tile(tile, rows=TILE):
    return pl.ds(pl.multiple_of(tile * rows, rows), rows)


def head_rows(ref, tile, heads):
    if heads == 1:
        return [ref[at_tile(tile), :]]
    own = ref.at[at_tile(tile, TILE * heads), :]
    return [own[pl.ds(h, TILE, stride=heads), :] for h in range(heads)]


def scale_of(before, tile, heads):
    token = lax.broadcasted_iota(jnp.int32, (1, TILE), 1) + (before + tile * TILE + 1)
    return beside([lax.rsqrt(token.astype(F32))] * heads)


def softmax_weights(chunk, part, heads, hd):
    scale = hd ** (-0.5) * 1.4426950408889634
    ahead = later_key_in_band(heads)
    span = TILE // heads
    skipped = part * (chunk.shape[0] - W)
    found = []
    for i, own in enumerate(columns(chunk)):
        a = skipped + i * span
        b = a + span
        rows = lambda start, stop: own[start - skipped : stop - skipped]
        edge = [rows(W, W + a)] * (a > 0) + [jnp.where(ahead, rows(a, b), rows(W + a, W + b))]
        edge = below(edge + [rows(b, TILE)] * (b < TILE))
        kept = [edge] + [rows(j * TILE, (j + 1) * TILE) for j in range(1, MIDS)]
        highest = jnp.max(functools.reduce(jnp.maximum, kept), axis=0, keepdims=True)
        kept = [jnp.exp2((p - highest) * scale) for p in kept]
        edge = kept[0]
        old = [jnp.zeros((a, TILE), BF16)] * (a > 0) + [jnp.where(ahead, edge[a:b], 0.0).astype(BF16)]
        new = [jnp.where(ahead, 0.0, edge[a:b]).astype(BF16)]
        if a > 0:
            new = [edge[:a].astype(BF16)] + new
        if b < TILE:
            old = old + [edge[b:].astype(BF16)]
            new = new + [jnp.zeros((TILE - b, TILE), BF16)]
        total = jnp.sum(functools.reduce(jnp.add, kept), axis=0, keepdims=True)
        found.append((below(old + [p.astype(BF16) for p in kept[1:]] + new), total))
    return beside([f[0] for f in found]), beside([f[1] for f in found])


def softmax_tiles(q_ref, k_ext, v_ext, out_ref, first_tile, tiles, heads, present, meanwhile, stored):
    hd = q_ref.shape[1]
    rows = TILE * heads
    lanes = min(2 * TILE, rows)
    span = lanes // heads

    chunks = rows // lanes
    units = tiles * chunks
    values = {}

    def scores(u):
        t, i = divmod(u, chunks)
        if t >= tiles:
            return None
        keys = k_ext[pl.ds(pl.multiple_of((first_tile + t) * TILE + i * span, span), W + span), :]
        queries = q_ref[pl.ds(pl.multiple_of((first_tile + t) * rows + i * lanes, lanes), lanes), :]
        return nt(keys, queries)

    def output(u, found):
        t, i = divmod(u, chunks)
        weights, total = found
        if i == 0:
            values[t] = beside([v_ext[first_tile + t + j] for j in range(MIDS + 1)])
            if present is not None and t < MIDS:
                ones = jnp.ones((ONES, TILE), BF16)
                sides = [present if t + j < MIDS else ones for j in range(MIDS + 1)]
                values[t] = below([values[t], beside(sides)])
        out = nn(values[t], weights)
        if present is not None and t < MIDS:
            total = out[hd : hd + 1]
        out = (out[:hd] * (1.0 / total)).astype(BF16).T
        out_ref[pl.ds(pl.multiple_of((first_tile + t) * rows + i * lanes, lanes), lanes), :] = out
        if i == chunks - 1:
            stored(t)

    ahead, behind = DEPTH * chunks, LATE * chunks
    now = {u: scores(u) for u in range(ahead)}
    if meanwhile is not None:
        meanwhile()
    found = {}
    for u in range(units):
        now[u + ahead] = scores(u + ahead)
        found[u] = softmax_weights(now.pop(u), u % chunks, heads, hd)
        if u >= behind:
            output(u - behind, found.pop(u - behind))
    for u in range(units - behind, units):
        output(u, found.pop(u))


def gradient_tiles(q_ref, c_ref, v_ref, kft, state, grad, before, first_tile, tiles):
    heads = grad.shape[0]
    ahead = later_key(heads)
    group = 2 if tiles % 2 == 0 else 1
    now = state[...]
    starts, turned, backs, found, q = {}, {}, {}, {}, {}

    def load(t, now):
        if t >= tiles:
            return now
        here = at_tile(first_tile + t)
        turned[t] = below(head_rows(c_ref, first_tile + t, heads)).T
        q[t] = head_rows(q_ref, first_tile + t, heads)
        starts[t] = now.astype(BF16)
        return now + nn(kft[:, here], v_ref[here, :])

    def score(t):
        if t < tiles:
            back = nn(v_ref[at_tile(first_tile + t), :], turned[t])
            backs[t] = jnp.where(ahead, 0.0, back).astype(BF16)

    def gradient(t):
        left = beside([kft[:, at_tile(first_tile + t)], starts[t]])
        out = nn(left, below([backs[t], turned[t]])) * scale_of(before, first_tile + t, heads)
        found[t] = columns(out.astype(BF16))

    def add(ts):
        for h in range(heads):
            grad[h] += nn(beside([found[t][h] for t in ts]), below([q[t][h] for t in ts]))

    for t in range(LAG + 1):
        now = load(t, now)
    for t in range(LAG):
        score(t)
    for t in range(tiles):
        now = load(t + LAG + 1, now)
        score(t + LAG)
        gradient(t)
        if t and t % group == 0:
            add(range(t - group, t))
    add(range(tiles - group, tiles))
    state[...] = now


def linear_tiles(q_ref, kf_ref, vt_ref, maps_t, state, out_ref, first_token):
    heads, hd = q_ref.shape[1:]
    tiles = q_ref.shape[0] // TILE
    ahead = later_key(heads)
    group = 2 if tiles % 2 == 0 else 1
    q = pltpu.einshape("tha->hta", q_ref[...])
    now = state[...]
    starts, turned, inside, done = {}, {}, {}, []

    def load(t, now):
        if t >= tiles:
            return now
        if t % group == 0:
            rows = slice(t * TILE, (t + group) * TILE)
            features = [columns(nt(maps_t[h], q[h, rows]).astype(BF16)) for h in range(heads)]
            for i in range(group):
                turned[t + i] = beside([f[i] for f in features])
        starts[t] = now.astype(BF16)
        return now + nn(vt_ref[t], kf_ref[at_tile(t), :])

    def score(t):
        if t < tiles:
            scores = nn(kf_ref[at_tile(t), :], turned[t])
            inside[t] = jnp.where(ahead, 0.0, scores).astype(BF16)

    def output(t):
        left = beside([vt_ref[t], starts[t]])
        out = nn(left, below([inside[t], turned[t]])) * scale_of(first_token, t, heads)
        done.append([x.T for x in columns(out.astype(BF16))])

    for t in range(LAG + 1):
        now = load(t, now)
    for t in range(LAG):
        score(t)
    for t in range(tiles):
        now = load(t + LAG + 1, now)
        score(t + LAG)
        output(t)
    state[...] = now
    out_ref[...] = pltpu.einshape("hta->tha", below([below([d[h] for d in done])[None] for h in range(heads)]))


def first_kernel(
    count, step_tiles,
    q_hbm, c_hbm, k_hbm, v_hbm, key_map_ref,
    soft_hbm, vt_hbm, prefix_ref, mine_ref,
    q_all, c_all, k_ext, v_all, v_ext, kft, soft_all,
    local_sum, sums, halo, state, grad, pieces, pieces16, slots,
    load_sem, store_sem, sum_send, sum_recv, halo_send, halo_recv, piece_send, piece_recv,
):
    rank = lax.axis_index("seq")
    heads, hd = grad.shape[:2]
    tokens_here = v_all.shape[0]
    blocks = tokens_here // TILE
    share = hd // count
    half = blocks // 2
    before = rank * tokens_here

    def halo_copy(i):
        return pltpu.make_async_remote_copy(
            src_ref=(k_ext.at[pl.ds(tokens_here, W)], v_all.at[pl.ds(tokens_here - W, W)])[i],
            dst_ref=halo.at[i],
            send_sem=halo_send.at[i],
            recv_sem=halo_recv.at[i],
            device_id={"seq": rank + 1},
            device_id_type=MESH,
        )

    def sum_copy(k):
        return pltpu.make_async_remote_copy(
            src_ref=local_sum,
            dst_ref=sums.at[k - 1],
            send_sem=sum_send.at[k - 1],
            recv_sem=sum_recv.at[k - 1],
            device_id={"seq": rank + k},
            device_id_type=MESH,
        )

    def piece_copy(k):
        target = lax.rem(rank + k, count)
        return pltpu.make_async_remote_copy(
            src_ref=pieces16.at[target],
            dst_ref=slots.at[k - 1],
            send_sem=piece_send.at[k - 1],
            recv_sem=piece_recv.at[k - 1],
            device_id={"seq": target},
            device_id_type=MESH,
        )

    rows = TILE * heads
    lead = 3 * step_tiles // 4
    grain = 2

    def tiles_of(first, tiles):
        return pl.ds(first * rows, tiles * rows)

    first_part, late, soon = tiles_of(half, lead), tiles_of(half + lead, blocks - half - lead), tiles_of(0, half)
    loads = [
        pltpu.make_async_copy(source, target, load_sem.at[i])
        for i, (source, target) in enumerate([
            (k_hbm, k_ext.at[pl.ds(W, tokens_here)]),
            (v_hbm, v_all),
            (q_hbm.at[first_part], q_all.at[first_part]),
            (q_hbm.at[late], q_all.at[late]),
            (c_hbm, c_all),
            (q_hbm.at[soon], q_all.at[soon]),
        ])
    ]

    def soft_store(i):
        part = tiles_of(i * grain, grain)
        return pltpu.make_async_copy(soft_all.at[part], soft_hbm.at[part], store_sem.at[i])

    def softmax(first_tile, tiles, present=None, meanwhile=None):
        def stored(t):
            if (t + 1) % grain == 0:
                soft_store((first_tile + t) // grain).start()

        softmax_tiles(q_all, k_ext, v_ext, soft_all, first_tile, tiles, heads, present, meanwhile, stored)

    barrier = pltpu.get_barrier_semaphore()
    for k in range(1, count):
        pl.semaphore_signal(barrier, inc=1, device_id={"seq": lax.rem(rank + k, count)}, device_id_type=MESH)
    for load in loads[:3]:
        load.start()
    grad[...] = jnp.zeros_like(grad)
    state[...] = jnp.zeros_like(state)
    for load in loads[3:]:
        load.start()
    key_map_t = key_map_ref[...].astype(F32).T.astype(BF16)
    loads[0].wait()
    kft[...] = nt(key_map_t, k_ext[W:]).astype(BF16)
    loads[1].wait()
    loads[2].wait()
    for b in range(blocks):
        v_ext[MIDS + b] = v_all[b * TILE : (b + 1) * TILE, :].T

    def shard_sum():
        near, far = slice(0, tokens_here // 2), slice(tokens_here // 2, tokens_here)
        local_sum[...] = (nn(kft[:, near], v_all[near, :]) + nn(kft[:, far], v_all[far, :])).astype(BF16)

    softmax(half, lead, meanwhile=shard_sum)
    vt_store = pltpu.make_async_copy(v_ext.at[pl.ds(MIDS, blocks)], vt_hbm, store_sem.at[blocks // grain])
    vt_store.start()

    pl.semaphore_wait(barrier, count - 1)
    for k in reversed(range(1, count)):
        @pl.when(rank + k < count)
        def _():
            sum_copy(k).start()

    loads[3].wait()
    softmax(half + lead, blocks - half - lead)

    for k in range(1, count):
        @pl.when(rank + k < count)
        def _():
            sum_copy(k).wait_send()
        @pl.when(rank >= k)
        def _():
            sum_copy(k).wait_recv()
            state[...] += sums[k - 1].astype(F32)
    @pl.when(rank + 1 < count)
    def _():
        halo_copy(0).start()
        halo_copy(1).start()
    prefix_ref[...] = state[...].T
    loads[4].wait()
    loads[5].wait()

    @pl.loop(0, blocks // (2 * step_tiles))
    def _(i):
        gradient_tiles(q_all, c_all, v_all, kft, state, grad, before, i * 2 * step_tiles, 2 * step_tiles)

    for h in range(heads):
        turned = grad[h].T
        for p in range(count):
            piece = turned[p * share : (p + 1) * share]
            pieces[p, :, h * hd : (h + 1) * hd] = piece
            pieces16[p, :, h * hd : (h + 1) * hd] = piece.astype(BF16)
    for k in reversed(range(1, count)):
        piece_copy(k).start()

    softmax(MIDS, half - MIDS)

    @pl.when(rank + 1 < count)
    def _():
        halo_copy(0).wait_send()
        halo_copy(1).wait_send()
    @pl.when(rank >= 1)
    def _():
        halo_copy(0).wait_recv()
        halo_copy(1).wait_recv()
        k_ext[:W] = halo[0]
        for b in range(MIDS):
            v_ext[b] = halo[1, b * TILE : (b + 1) * TILE, :].T
    @pl.when(rank == 0)
    def _():
        k_ext[:W] = jnp.broadcast_to(k_ext[W : W + 1, :], (W, hd))
        v_ext[:MIDS] = jnp.zeros((MIDS,) + v_ext.shape[1:], BF16)
    softmax(0, MIDS, jnp.where(rank == 0, jnp.zeros((ONES, TILE), F32), 1.0).astype(BF16))

    total = pieces[rank]
    for k in range(1, count):
        piece_copy(k).wait()
        total = total + slots[k - 1].astype(F32)
    mine_ref[...] = total
    for i in range(blocks // grain):
        soft_store(i).wait()
    vt_store.wait()


def last_kernel(
    steps,
    q_ref, k_first_ref, k_next_ref, vt_ref, soft_in_hbm, key_map_ref, maps_ref, prefix_ref, mine_in_ref,
    linear_ref, soft_hbm, mine_ref,
    kf, soft_all, maps_t, state, load_sem, store_sem,
):
    step = pl.program_id(0)
    heads, hd = q_ref.shape[1:]
    step_tokens = q_ref.shape[0]
    rows = step_tokens * heads

    def part(i):
        return pl.ds(pl.multiple_of(i * rows, rows), rows)

    def load(i):
        return pltpu.make_async_copy(soft_in_hbm.at[part(i)], soft_all.at[part(i)], load_sem.at[i])

    def store(i):
        return pltpu.make_async_copy(soft_all.at[part(i)], soft_hbm.at[part(i)], store_sem.at[i])

    @pl.when(step == 0)
    def _():
        for i in range(steps):
            load(i).start()
        kf[0] = nn(k_first_ref[...], key_map_ref[...]).astype(BF16)
        for h in range(heads):
            maps_t[h] = maps_ref[h].T
            mine_ref[:, h, :] = mine_in_ref[:, h * hd : (h + 1) * hd]
        state[...] = prefix_ref[...]

    @pl.when(step >= 1)
    def _():
        load(step - 1).wait()
        store(step - 1).start()

    @pl.when(step == steps - 1)
    def _():
        load(step).wait()
        store(step).start()

    first_token = (lax.axis_index("seq") * steps + step) * step_tokens
    linear_tiles(q_ref, kf.at[lax.rem(step, 2)], vt_ref, maps_t, state, linear_ref, first_token)
    kf[lax.rem(step + 1, 2)] = nn(k_next_ref[...], key_map_ref[...]).astype(BF16)

    @pl.when(step == steps - 1)
    def _():
        for i in range(steps):
            store(i).wait()


def per_device(queries, keys, values, query_maps, key_map, linear_cotangent):
    tokens_here, hd = keys.shape
    heads = queries.shape[1]
    count = lax.axis_size("seq")
    share = hd // count
    blocks = tokens_here // TILE
    step_tiles = 8
    steps = blocks // step_tiles
    flat = (tokens_here * heads, hd)
    dma = pltpu.SemaphoreType.DMA
    hbm = pl.BlockSpec(memory_space=pl.ANY)
    vmem = pl.BlockSpec(memory_space=pltpu.VMEM)

    rows16 = jax.ShapeDtypeStruct(flat, BF16)
    vt16 = jax.ShapeDtypeStruct((blocks, hd, TILE), BF16)
    square = jax.ShapeDtypeStruct((hd, hd), F32)
    piece = jax.ShapeDtypeStruct((share, heads * hd), F32)
    soft, values_t, prefix, mine = pl.pallas_call(
        functools.partial(first_kernel, count, step_tiles),
        in_specs=[hbm, hbm, hbm, hbm, vmem],
        out_specs=[hbm, hbm, vmem, vmem],
        out_shape=[rows16, vt16, square, piece],
        scratch_shapes=[
            pltpu.VMEM(flat, BF16),
            pltpu.VMEM(flat, BF16),
            pltpu.VMEM((tokens_here + W, hd), BF16),
            pltpu.VMEM((tokens_here, hd), BF16),
            pltpu.VMEM((blocks + MIDS, hd, TILE), BF16),
            pltpu.VMEM((hd, tokens_here), BF16),
            pltpu.VMEM(flat, BF16),
            pltpu.VMEM((hd, hd), BF16),
            pltpu.VMEM((count - 1, hd, hd), BF16),
            pltpu.VMEM((2, W, hd), BF16),
            pltpu.VMEM((hd, hd), F32),
            pltpu.VMEM((heads, hd, hd), F32),
            pltpu.VMEM((count, share, heads * hd), F32),
            pltpu.VMEM((count, share, heads * hd), BF16),
            pltpu.VMEM((count - 1, share, heads * hd), BF16),
            dma((6,)), dma((blocks // 2 + 1,)),
            dma((count - 1,)), dma((count - 1,)), dma((2,)), dma((2,)), dma((count - 1,)), dma((count - 1,)),
        ],
        compiler_params=pltpu.CompilerParams(collective_id=0, has_side_effects=True),
        name="softmax_and_gradient",
    )(queries.reshape(flat), linear_cotangent.reshape(flat), keys, values, key_map)

    once = lambda a: pl.BlockSpec(a.shape, lambda i: (0,) * len(a.shape), pipeline_mode=pl.Buffered(1))
    tokens = step_tiles * TILE
    along = pl.BlockSpec((tokens, heads, hd), lambda i: (i, 0, 0))
    final = jax.ShapeDtypeStruct((share, heads, hd), F32)
    linear, soft, mine = pl.pallas_call(
        functools.partial(last_kernel, steps),
        grid=(steps,),
        in_specs=[
            along,
            pl.BlockSpec((tokens, hd), lambda i: (0, 0), pipeline_mode=pl.Buffered(1)),
            pl.BlockSpec((tokens, hd), lambda i: (jnp.minimum(i + 1, steps - 1), 0)),
            pl.BlockSpec((step_tiles, hd, TILE), lambda i: (i, 0, 0)),
            hbm, once(key_map), once(query_maps), once(prefix), once(mine),
        ],
        out_specs=[along, hbm, once(final)],
        out_shape=[jax.ShapeDtypeStruct((tokens_here, heads, hd), BF16), rows16, final],
        scratch_shapes=[
            pltpu.VMEM((2, tokens, hd), BF16),
            pltpu.VMEM(flat, BF16),
            pltpu.VMEM((heads, hd, hd), BF16),
            pltpu.VMEM((hd, hd), F32),
            dma((steps,)), dma((steps,)),
        ],
        compiler_params=pltpu.CompilerParams(dimension_semantics=("arbitrary",)),
        name="linear",
    )(queries, keys, keys, values_t, soft, key_map, query_maps, prefix, mine)
    return soft.reshape(queries.shape), linear, mine


def solution(mesh):
    rows = P(("groups", "seq"), ("head", "rep"), None)
    return jax.shard_map(
        per_device,
        mesh=mesh,
        in_specs=(
            rows,
            P(("groups", "seq"), None),
            P(("groups", "seq"), None),
            P(("groups", "head", "rep"), None, None),
            P("groups", None),
            rows,
        ),
        out_specs=(rows, rows, rows),
        check_vma=False,
    )
```

```python
import functools

import jax
import jax.numpy as jnp
from jax import lax
from jax.experimental import pallas as pl
from jax.experimental.pallas import tpu as pltpu
from jax.sharding import PartitionSpec as P

W = 512
TILE = 128
MIDS = W // TILE
ONES = 16
LAG = 3
DEPTH = 2
LATE = 1
MESH = pl.DeviceIdType.MESH
F32 = jnp.float32
BF16 = jnp.bfloat16


def nt(a, b):
    return lax.dot_general(a, b, (((1,), (1,)), ((), ())), preferred_element_type=F32)


def nn(a, b):
    return jnp.dot(a, b, preferred_element_type=F32)


def beside(parts):
    return parts[0] if len(parts) == 1 else jnp.concatenate(parts, 1)


def below(parts):
    return parts[0] if len(parts) == 1 else jnp.concatenate(parts, 0)


def later_key(heads):
    shape = (TILE, TILE)
    one = lax.broadcasted_iota(jnp.int32, shape, 0) > lax.broadcasted_iota(jnp.int32, shape, 1)
    return beside([one] * heads)


def later_key_in_band(heads):
    shape = (TILE // heads, TILE)
    return lax.broadcasted_iota(jnp.int32, shape, 0) > lax.broadcasted_iota(jnp.int32, shape, 1) // heads


def columns(x):
    return [x[:, h : h + TILE] for h in range(0, x.shape[1], TILE)]


def at_tile(tile, rows=TILE):
    return pl.ds(pl.multiple_of(tile * rows, rows), rows)


def head_rows(ref, tile, heads):
    if heads == 1:
        return [ref[at_tile(tile), :]]
    own = ref.at[at_tile(tile, TILE * heads), :]
    return [own[pl.ds(h, TILE, stride=heads), :] for h in range(heads)]


def scale_of(before, tile, heads):
    token = lax.broadcasted_iota(jnp.int32, (1, TILE), 1) + (before + tile * TILE + 1)
    return beside([lax.rsqrt(token.astype(F32))] * heads)


def softmax_weights(chunk, part, heads, hd):
    scale = hd ** (-0.5) * 1.4426950408889634
    ahead = later_key_in_band(heads)
    span = TILE // heads
    skipped = part * (chunk.shape[0] - W)
    found = []
    for i, own in enumerate(columns(chunk)):
        a = skipped + i * span
        b = a + span
        rows = lambda start, stop: own[start - skipped : stop - skipped]
        edge = [rows(W, W + a)] * (a > 0) + [jnp.where(ahead, rows(a, b), rows(W + a, W + b))]
        edge = below(edge + [rows(b, TILE)] * (b < TILE))
        kept = [edge] + [rows(j * TILE, (j + 1) * TILE) for j in range(1, MIDS)]
        highest = jnp.max(functools.reduce(jnp.maximum, kept), axis=0, keepdims=True)
        kept = [jnp.exp2((p - highest) * scale) for p in kept]
        edge = kept[0]
        old = [jnp.zeros((a, TILE), BF16)] * (a > 0) + [jnp.where(ahead, edge[a:b], 0.0).astype(BF16)]
        new = [jnp.where(ahead, 0.0, edge[a:b]).astype(BF16)]
        if a > 0:
            new = [edge[:a].astype(BF16)] + new
        if b < TILE:
            old = old + [edge[b:].astype(BF16)]
            new = new + [jnp.zeros((TILE - b, TILE), BF16)]
        total = jnp.sum(functools.reduce(jnp.add, kept), axis=0, keepdims=True)
        found.append((below(old + [p.astype(BF16) for p in kept[1:]] + new), total))
    return beside([f[0] for f in found]), beside([f[1] for f in found])


def softmax_tiles(q_ref, k_ext, v_ext, out_ref, first_tile, tiles, heads, present, meanwhile, stored):
    hd = q_ref.shape[1]
    rows = TILE * heads
    lanes = min(2 * TILE, rows)
    span = lanes // heads

    chunks = rows // lanes
    units = tiles * chunks
    values = {}

    def scores(u):
        t, i = divmod(u, chunks)
        if t >= tiles:
            return None
        keys = k_ext[pl.ds(pl.multiple_of((first_tile + t) * TILE + i * span, span), W + span), :]
        queries = q_ref[pl.ds(pl.multiple_of((first_tile + t) * rows + i * lanes, lanes), lanes), :]
        return nt(keys, queries)

    def output(u, found):
        t, i = divmod(u, chunks)
        weights, total = found
        if i == 0:
            values[t] = beside([v_ext[first_tile + t + j] for j in range(MIDS + 1)])
            if present is not None and t < MIDS:
                ones = jnp.ones((ONES, TILE), BF16)
                sides = [present if t + j < MIDS else ones for j in range(MIDS + 1)]
                values[t] = below([values[t], beside(sides)])
        out = nn(values[t], weights)
        if present is not None and t < MIDS:
            total = out[hd : hd + 1]
        out = (out[:hd] * (1.0 / total)).astype(BF16).T
        out_ref[pl.ds(pl.multiple_of((first_tile + t) * rows + i * lanes, lanes), lanes), :] = out
        if i == chunks - 1:
            stored(t)

    ahead, behind = DEPTH * chunks, LATE * chunks
    now = {u: scores(u) for u in range(ahead)}
    if meanwhile is not None:
        meanwhile()
    found = {}
    for u in range(units):
        now[u + ahead] = scores(u + ahead)
        found[u] = softmax_weights(now.pop(u), u % chunks, heads, hd)
        if u >= behind:
            output(u - behind, found.pop(u - behind))
    for u in range(units - behind, units):
        output(u, found.pop(u))


def gradient_tiles(q_ref, c_ref, v_ref, kft, state, grad, before, first_tile, tiles):
    heads = grad.shape[0]
    ahead = later_key(heads)
    group = 2 if tiles % 2 == 0 else 1
    now = state[...]
    starts, turned, backs, found, q = {}, {}, {}, {}, {}

    def load(t, now):
        if t >= tiles:
            return now
        here = at_tile(first_tile + t)
        turned[t] = below(head_rows(c_ref, first_tile + t, heads)).T
        q[t] = head_rows(q_ref, first_tile + t, heads)
        starts[t] = now.astype(BF16)
        return now + nn(kft[:, here], v_ref[here, :])

    def score(t):
        if t < tiles:
            back = nn(v_ref[at_tile(first_tile + t), :], turned[t])
            backs[t] = jnp.where(ahead, 0.0, back).astype(BF16)

    def gradient(t):
        left = beside([kft[:, at_tile(first_tile + t)], starts[t]])
        out = nn(left, below([backs[t], turned[t]])) * scale_of(before, first_tile + t, heads)
        found[t] = columns(out.astype(BF16))

    def add(ts):
        for h in range(heads):
            grad[h] += nn(beside([found[t][h] for t in ts]), below([q[t][h] for t in ts]))

    for t in range(LAG + 1):
        now = load(t, now)
    for t in range(LAG):
        score(t)
    for t in range(tiles):
        now = load(t + LAG + 1, now)
        score(t + LAG)
        gradient(t)
        if t and t % group == 0:
            add(range(t - group, t))
    add(range(tiles - group, tiles))
    state[...] = now


def linear_tiles(q_ref, kf_ref, vt_ref, maps_t, state, out_ref, first_token):
    heads, hd = q_ref.shape[1:]
    tiles = q_ref.shape[0] // TILE
    ahead = later_key(heads)
    group = 2 if tiles % 2 == 0 else 1
    q = pltpu.einshape("tha->hta", q_ref[...])
    now = state[...]
    starts, turned, inside, done = {}, {}, {}, []

    def load(t, now):
        if t >= tiles:
            return now
        if t % group == 0:
            rows = slice(t * TILE, (t + group) * TILE)
            features = [columns(nt(maps_t[h], q[h, rows]).astype(BF16)) for h in range(heads)]
            for i in range(group):
                turned[t + i] = beside([f[i] for f in features])
        starts[t] = now.astype(BF16)
        return now + nn(vt_ref[t], kf_ref[at_tile(t), :])

    def score(t):
        if t < tiles:
            scores = nn(kf_ref[at_tile(t), :], turned[t])
            inside[t] = jnp.where(ahead, 0.0, scores).astype(BF16)

    def output(t):
        left = beside([vt_ref[t], starts[t]])
        out = nn(left, below([inside[t], turned[t]])) * scale_of(first_token, t, heads)
        done.append([x.T for x in columns(out.astype(BF16))])

    for t in range(LAG + 1):
        now = load(t, now)
    for t in range(LAG):
        score(t)
    for t in range(tiles):
        now = load(t + LAG + 1, now)
        score(t + LAG)
        output(t)
    state[...] = now
    out_ref[...] = pltpu.einshape("hta->tha", below([below([d[h] for d in done])[None] for h in range(heads)]))


def first_kernel(
    count, step_tiles,
    q_hbm, c_hbm, k_hbm, v_hbm, key_map_ref,
    soft_hbm, vt_hbm, prefix_ref, mine_ref,
    q_all, c_all, k_ext, v_all, v_ext, kft, soft_all,
    local_sum, sums, halo, state, grad, pieces, pieces16, slots,
    load_sem, store_sem, sum_send, sum_recv, halo_send, halo_recv, piece_send, piece_recv,
):
    rank = lax.axis_index("seq")
    heads, hd = grad.shape[:2]
    tokens_here = v_all.shape[0]
    blocks = tokens_here // TILE
    share = hd // count
    half = blocks // 2 + 2
    before = rank * tokens_here

    def halo_copy(i):
        return pltpu.make_async_remote_copy(
            src_ref=(k_ext.at[pl.ds(tokens_here, W)], v_all.at[pl.ds(tokens_here - W, W)])[i],
            dst_ref=halo.at[i],
            send_sem=halo_send.at[i],
            recv_sem=halo_recv.at[i],
            device_id={"seq": rank + 1},
            device_id_type=MESH,
        )

    def sum_copy(k):
        return pltpu.make_async_remote_copy(
            src_ref=local_sum,
            dst_ref=sums.at[k - 1],
            send_sem=sum_send.at[k - 1],
            recv_sem=sum_recv.at[k - 1],
            device_id={"seq": rank + k},
            device_id_type=MESH,
        )

    def piece_copy(k):
        target = lax.rem(rank + k, count)
        return pltpu.make_async_remote_copy(
            src_ref=pieces16.at[target],
            dst_ref=slots.at[k - 1],
            send_sem=piece_send.at[k - 1],
            recv_sem=piece_recv.at[k - 1],
            device_id={"seq": target},
            device_id_type=MESH,
        )

    rows = TILE * heads
    lead = step_tiles // 2
    grain = 2

    def tiles_of(first, tiles):
        return pl.ds(first * rows, tiles * rows)

    first_part, late, soon = tiles_of(half, lead), tiles_of(half + lead, blocks - half - lead), tiles_of(0, half)
    loads = [
        pltpu.make_async_copy(source, target, load_sem.at[i])
        for i, (source, target) in enumerate([
            (k_hbm, k_ext.at[pl.ds(W, tokens_here)]),
            (v_hbm, v_all),
            (q_hbm.at[first_part], q_all.at[first_part]),
            (q_hbm.at[late], q_all.at[late]),
            (c_hbm, c_all),
            (q_hbm.at[soon], q_all.at[soon]),
        ])
    ]

    def soft_store(i):
        part = tiles_of(i * grain, grain)
        return pltpu.make_async_copy(soft_all.at[part], soft_hbm.at[part], store_sem.at[i])

    def softmax(first_tile, tiles, present=None, meanwhile=None):
        def stored(t):
            if (t + 1) % grain == 0:
                soft_store((first_tile + t) // grain).start()

        softmax_tiles(q_all, k_ext, v_ext, soft_all, first_tile, tiles, heads, present, meanwhile, stored)

    barrier = pltpu.get_barrier_semaphore()
    for k in range(1, count):
        pl.semaphore_signal(barrier, inc=1, device_id={"seq": lax.rem(rank + k, count)}, device_id_type=MESH)
    for load in loads[:3]:
        load.start()
    grad[...] = jnp.zeros_like(grad)
    state[...] = jnp.zeros_like(state)
    for load in loads[3:]:
        load.start()
    key_map_t = key_map_ref[...].astype(F32).T.astype(BF16)
    loads[0].wait()
    kft[...] = nt(key_map_t, k_ext[W:]).astype(BF16)
    loads[1].wait()
    loads[2].wait()
    for b in range(blocks):
        v_ext[MIDS + b] = v_all[b * TILE : (b + 1) * TILE, :].T

    def shard_sum():
        near, far = slice(0, tokens_here // 2), slice(tokens_here // 2, tokens_here)
        local_sum[...] = (nn(kft[:, near], v_all[near, :]) + nn(kft[:, far], v_all[far, :])).astype(BF16)

    softmax(half, lead, meanwhile=shard_sum)
    vt_store = pltpu.make_async_copy(v_ext.at[pl.ds(MIDS, blocks)], vt_hbm, store_sem.at[blocks // grain])
    vt_store.start()

    pl.semaphore_wait(barrier, count - 1)
    for k in reversed(range(1, count)):
        @pl.when(rank + k < count)
        def _():
            sum_copy(k).start()

    loads[3].wait()
    softmax(half + lead, blocks - half - lead)

    for k in range(1, count):
        @pl.when(rank + k < count)
        def _():
            sum_copy(k).wait_send()
        @pl.when(rank >= k)
        def _():
            sum_copy(k).wait_recv()
            state[...] += sums[k - 1].astype(F32)
    @pl.when(rank + 1 < count)
    def _():
        halo_copy(0).start()
        halo_copy(1).start()
    prefix_ref[...] = state[...].T
    loads[4].wait()
    loads[5].wait()

    @pl.loop(0, blocks // (2 * step_tiles))
    def _(i):
        gradient_tiles(q_all, c_all, v_all, kft, state, grad, before, i * 2 * step_tiles, 2 * step_tiles)

    for h in range(heads):
        turned = grad[h].T
        for p in range(count):
            piece = turned[p * share : (p + 1) * share]
            pieces[p, :, h * hd : (h + 1) * hd] = piece
            pieces16[p, :, h * hd : (h + 1) * hd] = piece.astype(BF16)
    for k in range(1, count):
        piece_copy(k).start()

    softmax(MIDS, half - MIDS)

    @pl.when(rank + 1 < count)
    def _():
        halo_copy(0).wait_send()
        halo_copy(1).wait_send()
    @pl.when(rank >= 1)
    def _():
        halo_copy(0).wait_recv()
        halo_copy(1).wait_recv()
        k_ext[:W] = halo[0]
        for b in range(MIDS):
            v_ext[b] = halo[1, b * TILE : (b + 1) * TILE, :].T
    @pl.when(rank == 0)
    def _():
        k_ext[:W] = jnp.broadcast_to(k_ext[W : W + 1, :], (W, hd))
        v_ext[:MIDS] = jnp.zeros((MIDS,) + v_ext.shape[1:], BF16)
    softmax(0, MIDS, jnp.where(rank == 0, jnp.zeros((ONES, TILE), F32), 1.0).astype(BF16))

    total = pieces[rank]
    for k in range(1, count):
        piece_copy(k).wait()
        total = total + slots[k - 1].astype(F32)
    mine_ref[...] = total
    for i in range(blocks // grain):
        soft_store(i).wait()
    vt_store.wait()


def last_kernel(
    steps,
    q_ref, k_first_ref, k_next_ref, vt_ref, soft_in_hbm, key_map_ref, maps_ref, prefix_ref, mine_in_ref,
    linear_ref, soft_hbm, mine_ref,
    kf, soft_all, maps_t, state, load_sem, store_sem,
):
    step = pl.program_id(0)
    heads, hd = q_ref.shape[1:]
    step_tokens = q_ref.shape[0]
    rows = step_tokens * heads

    def part(i):
        return pl.ds(pl.multiple_of(i * rows, rows), rows)

    def load(i):
        return pltpu.make_async_copy(soft_in_hbm.at[part(i)], soft_all.at[part(i)], load_sem.at[i])

    def store(i):
        return pltpu.make_async_copy(soft_all.at[part(i)], soft_hbm.at[part(i)], store_sem.at[i])

    @pl.when(step == 0)
    def _():
        for i in range(steps):
            load(i).start()
        kf[0] = nn(k_first_ref[...], key_map_ref[...]).astype(BF16)
        for h in range(heads):
            maps_t[h] = maps_ref[h].T
            mine_ref[:, h, :] = mine_in_ref[:, h * hd : (h + 1) * hd]
        state[...] = prefix_ref[...]

    @pl.when(step >= 1)
    def _():
        load(step - 1).wait()
        store(step - 1).start()

    @pl.when(step == steps - 1)
    def _():
        load(step).wait()
        store(step).start()

    first_token = (lax.axis_index("seq") * steps + step) * step_tokens
    linear_tiles(q_ref, kf.at[lax.rem(step, 2)], vt_ref, maps_t, state, linear_ref, first_token)
    kf[lax.rem(step + 1, 2)] = nn(k_next_ref[...], key_map_ref[...]).astype(BF16)

    @pl.when(step == steps - 1)
    def _():
        for i in range(steps):
            store(i).wait()


def per_device(queries, keys, values, query_maps, key_map, linear_cotangent):
    tokens_here, hd = keys.shape
    heads = queries.shape[1]
    count = lax.axis_size("seq")
    share = hd // count
    blocks = tokens_here // TILE
    step_tiles = 8
    steps = blocks // step_tiles
    flat = (tokens_here * heads, hd)
    dma = pltpu.SemaphoreType.DMA
    hbm = pl.BlockSpec(memory_space=pl.ANY)
    vmem = pl.BlockSpec(memory_space=pltpu.VMEM)

    rows16 = jax.ShapeDtypeStruct(flat, BF16)
    vt16 = jax.ShapeDtypeStruct((blocks, hd, TILE), BF16)
    square = jax.ShapeDtypeStruct((hd, hd), F32)
    piece = jax.ShapeDtypeStruct((share, heads * hd), F32)
    soft, values_t, prefix, mine = pl.pallas_call(
        functools.partial(first_kernel, count, step_tiles),
        in_specs=[hbm, hbm, hbm, hbm, vmem],
        out_specs=[hbm, hbm, vmem, vmem],
        out_shape=[rows16, vt16, square, piece],
        scratch_shapes=[
            pltpu.VMEM(flat, BF16),
            pltpu.VMEM(flat, BF16),
            pltpu.VMEM((tokens_here + W, hd), BF16),
            pltpu.VMEM((tokens_here, hd), BF16),
            pltpu.VMEM((blocks + MIDS, hd, TILE), BF16),
            pltpu.VMEM((hd, tokens_here), BF16),
            pltpu.VMEM(flat, BF16),
            pltpu.VMEM((hd, hd), BF16),
            pltpu.VMEM((count - 1, hd, hd), BF16),
            pltpu.VMEM((2, W, hd), BF16),
            pltpu.VMEM((hd, hd), F32),
            pltpu.VMEM((heads, hd, hd), F32),
            pltpu.VMEM((count, share, heads * hd), F32),
            pltpu.VMEM((count, share, heads * hd), BF16),
            pltpu.VMEM((count - 1, share, heads * hd), BF16),
            dma((6,)), dma((blocks // 2 + 1,)),
            dma((count - 1,)), dma((count - 1,)), dma((2,)), dma((2,)), dma((count - 1,)), dma((count - 1,)),
        ],
        compiler_params=pltpu.CompilerParams(collective_id=0, has_side_effects=True),
        name="softmax_and_gradient",
    )(queries.reshape(flat), linear_cotangent.reshape(flat), keys, values, key_map)

    once = lambda a: pl.BlockSpec(a.shape, lambda i: (0,) * len(a.shape), pipeline_mode=pl.Buffered(1))
    tokens = step_tiles * TILE
    along = pl.BlockSpec((tokens, heads, hd), lambda i: (i, 0, 0))
    final = jax.ShapeDtypeStruct((share, heads, hd), F32)
    linear, soft, mine = pl.pallas_call(
        functools.partial(last_kernel, steps),
        grid=(steps,),
        in_specs=[
            along,
            pl.BlockSpec((tokens, hd), lambda i: (0, 0), pipeline_mode=pl.Buffered(1)),
            pl.BlockSpec((tokens, hd), lambda i: (jnp.minimum(i + 1, steps - 1), 0)),
            pl.BlockSpec((step_tiles, hd, TILE), lambda i: (i, 0, 0)),
            hbm, once(key_map), once(query_maps), once(prefix), once(mine),
        ],
        out_specs=[along, hbm, once(final)],
        out_shape=[jax.ShapeDtypeStruct((tokens_here, heads, hd), BF16), rows16, final],
        scratch_shapes=[
            pltpu.VMEM((2, tokens, hd), BF16),
            pltpu.VMEM(flat, BF16),
            pltpu.VMEM((heads, hd, hd), BF16),
            pltpu.VMEM((hd, hd), F32),
            dma((steps,)), dma((steps,)),
        ],
        compiler_params=pltpu.CompilerParams(dimension_semantics=("arbitrary",)),
        name="linear",
    )(queries, keys, keys, values_t, soft, key_map, query_maps, prefix, mine)
    return soft.reshape(queries.shape), linear, mine


def solution(mesh):
    rows = P(("groups", "seq"), ("head", "rep"), None)
    return jax.shard_map(
        per_device,
        mesh=mesh,
        in_specs=(
            rows,
            P(("groups", "seq"), None),
            P(("groups", "seq"), None),
            P(("groups", "head", "rep"), None, None),
            P("groups", None),
            rows,
        ),
        out_specs=(rows, rows, rows),
        check_vma=False,
    )
```
